32 devices in a mesh: helper: 16 (over z, x, core), tensor: 2 (over y).
Axes of the slice: x: 2, y: 2, z: 4, core: 2. Of those that a mesh axis runs over, the one named last changes fastest.
Arguments:
- recorded_input_rows: bfloat16 [16384, 2048], P('helper'), may hold values from -8 to 8
- out_cotangent: bfloat16 [16384, 2048], P('helper'), may hold values from -0.875 to 0.875
- fresh_rows: bfloat16 [4096, 2048], P('helper'), may hold values from -6 to 6
- seq_counts: int32 [16], replicated, may hold values from 1 to 4, 24 in all
- decay_logs: float32 [16, 256], P('tensor'), may hold values from -3 to 0
- norm_gain: float32 [2048], P('tensor'), may hold values from 0.25 to 1.75
- qkv_weight: float32 [2048, 3, 2048], P('helper', None, 'tensor'), may hold values from -0.125 to 0.125
- emitted_projection_matrix: float32 [2048, 2048], P('helper', 'tensor'), may hold values from -0.125 to 0.125
- qkv_first: float32 [2048, 3, 2048], P('helper', None, 'tensor'), may hold values from -6 to 6
- qkv_second: float32 [2048, 3, 2048], P('helper', None, 'tensor'), may hold values from 1 to 100
- out_first: float32 [2048, 2048], P('helper', 'tensor'), may hold values from -6 to 6
- out_second: float32 [2048, 2048], P('helper', 'tensor'), may hold values from 1 to 100
Outputs:
- fresh_out: bfloat16 [4096, 2048], P('helper')
- qkv_moment: float32 [2048, 3, 2048], P('helper', None, 'tensor')
- out_moment: float32 [2048, 2048], P('helper', 'tensor')
The draws below stay inside these ranges and needn't reach their ends.
Inputs may be any that keep to these rules, and one draw needn't show every extreme that they name: Helper h's live sequences are its first seq_counts[h] slots; the counts sum to three halves of the number of helpers, and the largest equals 4.
All inputs are finite; a program needn't handle non-finite values.
Results may differ from the reference program's by a relative error of at most 0.0095.
The reference program's roundings to bfloat16 on the way count: a program that leaves them out, or rounds other values in their place, can miss the bound.
Values may be sent and summed in bfloat16 or wider, within the bound.
A program may use at most 128 MiB of HBM per device.

```python
import math
import jax
import jax.numpy as jnp
import numpy as np
from jax import lax

HEADS = 16
D = 2048
SEQ_LEN = 256
SEQ_CAP = 4
N_HELPER = 16


def draw_decay_logs(key, part):
    key_rate = jax.random.fold_in(key, 11)
    key_place = jax.random.fold_in(key, 12)
    key_loss = jax.random.fold_in(key, 13)
    low_log = jnp.log(0.1 / SEQ_LEN)
    high_log = jnp.log(1.0 / 30.0)
    channel_fading_multiplier = jnp.exp(jax.random.uniform(key_rate, (HEADS, 1), jnp.float32, low_log, high_log))
    bucket_addresses = jax.random.randint(key_place, (HEADS, 3), 0, SEQ_LEN)
    objective_readings = jax.random.uniform(key_loss, (HEADS, 3), jnp.float32, 0.2, 0.5)
    element_indices = jnp.arange(SEQ_LEN)
    run_extent_list = jnp.sum(jnp.where(element_indices[None, None, :] == bucket_addresses[:, :, None], jnp.log(1.0 - objective_readings)[:, :, None], 0.0), axis=1)
    return (run_extent_list - channel_fading_multiplier).astype(jnp.float32)


def with_spikes(drawn, rng, source, target, parts, factor):
    owner, partner = [(jnp.arange(drawn.shape[position]) // (drawn.shape[position] // parts)).reshape([-1 if axis == position else 1 for axis in range(drawn.ndim)]) for position in (source, target)]
    chosen = jax.random.permutation(rng, parts)[partner]
    strong = (owner == chosen) | (owner == (partner + parts // 2) % parts)
    return jnp.where(strong, factor * drawn, drawn)


def shard_levels(stream_key, shape, cuts, smallest, high):
    gain = 1.0
    for dim, blocks in cuts:
        steps = jax.random.uniform(jax.random.fold_in(jax.random.fold_in(stream_key, 6), dim), (blocks,), jnp.float32, smallest / len(cuts), high / len(cuts))
        gain = gain * jnp.repeat(jnp.exp(steps), shape[dim] // blocks).reshape((-1,) + (1,) * (len(shape) - 1 - dim))
    return gain


def profile(count, total, bound, lean):
    loads = [(1 << 20) // math.isqrt(rank ** lean) + 1 for rank in range(2, count + 1)]
    rest, given = total - bound - (count - 1), [1] * (count - 1)
    while rest > 0:
        movable = [i for i in range(count - 1) if given[i] < bound]
        pool, left = sum([loads[i] for i in movable]), rest
        for i in movable:
            extra = min(bound - given[i], max(1, left * loads[i] // pool), rest)
            given[i] = given[i] + extra
            rest = rest - extra
    return np.array([bound] + given)


def uneven_parts(rng, count, total, limit, skew):
    if count == 2:
        one = jax.random.randint(rng, (), max(1, total - limit), min(limit, total - 1) + 1)
        return jnp.stack([one, total - one])
    sizes = jnp.asarray(profile(count, total, limit, skew), jnp.int32)
    twos = (count - 1) // 2
    donor, receiver = sizes[1:1 + 2 * twos:2], sizes[2:2 + 2 * twos:2]
    margin = jnp.minimum(donor - 1, limit - receiver)
    moved = jax.random.randint(jax.random.fold_in(rng, 1), (twos,), 0, 1 << 20) % (margin + 1)
    sizes = sizes.at[1:1 + 2 * twos:2].set(donor - moved).at[2:2 + 2 * twos:2].set(receiver + moved)
    return sizes[jax.random.permutation(jax.random.fold_in(rng, 2), count)]


def scatter_about(stream_key, extent, deviation, bound, cuts=(), kind=jnp.bfloat16):
    result = deviation * jax.random.normal(stream_key, extent, jnp.float32)
    if cuts:
        result = result * shard_levels(stream_key, extent, cuts, -0.22, 0.18)
    return jnp.clip(result, -bound, bound).astype(kind)


def heavy_noise(stream_key, shape, deviation, reach, shards, heavy, held_as=jnp.bfloat16):
    values = deviation * jax.random.normal(stream_key, shape, jnp.float32)
    if shards:
        values = values * shard_levels(stream_key, shape, shards, -0.22, 0.18)
    return jnp.clip(with_spikes(values, jax.random.fold_in(stream_key, 3), *heavy), -reach, reach).astype(held_as)


def setup_inputs(seed: int = 0) -> dict:
    key_list = jax.random.split(jax.random.key(seed), 13)
    recorded_input_rows = heavy_noise(key_list[0], (N_HELPER * SEQ_CAP * SEQ_LEN, D), 1.0, 8.0, ((0, 16),), (0, 1, 16, 2.0))
    out_cotangent = heavy_noise(key_list[1], (N_HELPER * SEQ_CAP * SEQ_LEN, D), 0.1, 0.875, ((0, 16),), (0, 1, 16, 2.0))
    fresh_rows = scatter_about(key_list[2], (N_HELPER * SEQ_LEN, D), 1.0, 6.0, ((0, 16),))
    seq_counts = uneven_parts(key_list[3], N_HELPER, 3 * N_HELPER // 2, SEQ_CAP, 2).astype(jnp.int32)
    decay_logs = draw_decay_logs(jax.random.fold_in(key_list[12], 71), 0)
    norm_gain = jnp.clip(1.0 + 0.15 * jax.random.normal(key_list[5], (D,), jnp.float32), 0.25, 1.75)
    qkv_weight = scatter_about(key_list[6], (D, 3, D), D ** -0.5, 0.125, ((0, 16), (2, 2)), jnp.float32)
    emitted_projection_matrix = scatter_about(key_list[7], (D, D), D ** -0.5, 0.125, ((0, 16), (1, 2)), jnp.float32)
    qkv_first = scatter_about(key_list[8], (D, 3, D), 1.0, 6.0, ((0, 16), (2, 2)), jnp.float32)
    qkv_second = jnp.clip(jnp.exp(math.log(100.0) - 4.6051702 * jax.random.uniform(key_list[9], (D, 3, D), jnp.float32) ** shard_levels(key_list[9], (D, 3, D), ((0, 16), (2, 2)), -0.2, 0.2)), 1.0, 100.0)
    out_first = scatter_about(key_list[10], (D, D), 1.0, 6.0, ((0, 16), (1, 2)), jnp.float32)
    out_second = jnp.clip(jnp.exp(math.log(100.0) - 4.6051702 * jax.random.uniform(key_list[11], (D, D), jnp.float32) ** shard_levels(key_list[11], (D, D), ((0, 16), (1, 2)), -0.2, 0.2)), 1.0, 100.0)
    return dict(recorded_input_rows=recorded_input_rows, out_cotangent=out_cotangent, fresh_rows=fresh_rows, seq_counts=seq_counts, decay_logs=decay_logs, norm_gain=norm_gain, qkv_weight=qkv_weight, emitted_projection_matrix=emitted_projection_matrix, qkv_first=qkv_first, qkv_second=qkv_second, out_first=out_first, out_second=out_second)


NORM_FLOOR = 1.0
BETA_ONE = 0.9
BETA_TWO = 0.95
ADAM_EPS = 1e-08
LEARN_RATE = 0.005
WEIGHT_DECAY = 0.1
BIAS_ONE = 0.9999734386011124
BIAS_TWO = 0.994079470779666

def product_of(form, left, right):
    return jnp.einsum(form, left.astype(jnp.float32), right.astype(jnp.float32))

def decay_table(decay_logs):
    running = jnp.cumsum(decay_logs.astype(jnp.float32), axis=1)
    length = decay_logs.shape[1]
    later = (jnp.arange(length)[:, None] >= jnp.arange(length)[None, :])[None]
    spread_factor = running[:, :, None] - running[:, None, :]
    return jnp.where(later, jnp.exp(jnp.where(later, spread_factor, 0.0)), 0.0)

def attend(projected, decay_mask, norm_gain):
    head_count = decay_mask.shape[0]
    split_shape = (projected.shape[0], projected.shape[1], head_count, projected.shape[3] // head_count)
    raw_query = projected[:, :, 0].reshape(split_shape)
    raw_key = projected[:, :, 1].reshape(split_shape)
    queries = (raw_query * jax.nn.sigmoid(raw_query)).astype(jnp.bfloat16)
    key_rows = (raw_key * jax.nn.sigmoid(raw_key)).astype(jnp.bfloat16)
    values = projected[:, :, 2].reshape(split_shape).astype(jnp.bfloat16)
    scores = product_of('sthd,suhd->shtu', queries, key_rows)
    weights = (scores * decay_mask[None]).astype(jnp.bfloat16)
    mixed = product_of('shtu,suhd->sthd', weights, values)
    mean_square = lax.optimization_barrier(jnp.mean(mixed * mixed, axis=-1, keepdims=True))
    active = jnp.where(mean_square > NORM_FLOOR, 1.0, 0.0)
    inverse = lax.rsqrt(jnp.maximum(mean_square, NORM_FLOOR))
    gain_heads = norm_gain.reshape(head_count, -1)
    attended = (mixed * inverse * gain_heads).astype(jnp.bfloat16)
    return (attended, (raw_query, raw_key, queries, key_rows, values, weights, mixed, inverse, active))

def attend_back(grad_attended, stashed, decay_mask, norm_gain):
    raw_query, raw_key, queries, key_rows, values, weights, mixed, inverse, active = stashed
    gain_heads = norm_gain.reshape(decay_mask.shape[0], -1)
    scaled = grad_attended * gain_heads
    grad_mixed = inverse * scaled - active * mixed * (inverse * inverse * inverse) * lax.optimization_barrier(jnp.mean(scaled * mixed, axis=-1, keepdims=True))
    grad_mixed = grad_mixed.astype(jnp.bfloat16)
    grad_weights = product_of('sthd,suhd->shtu', grad_mixed, values)
    grad_values = product_of('shtu,sthd->suhd', weights, grad_mixed)
    grad_scores = (grad_weights * decay_mask[None]).astype(jnp.bfloat16)
    grad_query = product_of('shtu,suhd->sthd', grad_scores, key_rows)
    grad_key = product_of('shtu,sthd->suhd', grad_scores, queries)
    sigma_query = jax.nn.sigmoid(raw_query)
    sigma_key = jax.nn.sigmoid(raw_key)
    grad_query = grad_query * sigma_query * (1.0 + raw_query * (1.0 - sigma_query))
    grad_key = grad_key * sigma_key * (1.0 + raw_key * (1.0 - sigma_key))
    return jnp.stack([grad_query, grad_key, grad_values], axis=2)

def adam_step(weight, first_moment, second_moment, gradient):
    first_new = BETA_ONE * first_moment + (1.0 - BETA_ONE) * gradient
    second_new = BETA_TWO * second_moment + (1.0 - BETA_TWO) * gradient * gradient
    update = first_new / BIAS_ONE / (jnp.sqrt(second_new / BIAS_TWO) + ADAM_EPS)
    weight_new = weight - LEARN_RATE * (update + WEIGHT_DECAY * weight)
    return (weight_new.astype(jnp.bfloat16), first_new)

def reference(recorded_input_rows, out_cotangent, fresh_rows, seq_counts, decay_logs, norm_gain, qkv_weight, emitted_projection_matrix, qkv_first, qkv_second, out_first, out_second):
    decay_mask = decay_table(decay_logs)
    model_width = qkv_weight.shape[0]
    head_count = decay_logs.shape[0]
    slot_total = recorded_input_rows.shape[0] // SEQ_LEN
    old_qkv = qkv_weight.astype(jnp.bfloat16).reshape(model_width, 3 * model_width)
    old_out = emitted_projection_matrix.astype(jnp.bfloat16)
    slot_index = (jnp.arange(slot_total) % SEQ_CAP).astype(jnp.int32)
    slot_limit = jnp.repeat(seq_counts.astype(jnp.int32), SEQ_CAP)
    slot_live = (slot_index < slot_limit).astype(jnp.float32)
    logged_seqs = recorded_input_rows.reshape(slot_total, SEQ_LEN, model_width)
    cot_seqs = out_cotangent.reshape(slot_total, SEQ_LEN, model_width)

    def replay_one(totals, inputs):
        seq_rows, seq_cot, live_flag = inputs

        def live_branch(partial_sums):
            projected = jnp.dot(seq_rows, old_qkv, preferred_element_type=jnp.float32).reshape(1, SEQ_LEN, 3, model_width)
            attended, stashed = attend(projected, decay_mask, norm_gain)
            grad_attended = jnp.dot(seq_cot, old_out, preferred_element_type=jnp.float32).reshape(1, SEQ_LEN, head_count, -1)
            grad_projected = attend_back(grad_attended, stashed, decay_mask, norm_gain)
            grad_projected = grad_projected.reshape(SEQ_LEN, 3 * model_width).astype(jnp.bfloat16)
            qkv_sum = partial_sums[0] + jnp.dot(seq_rows.T, grad_projected, preferred_element_type=jnp.float32)
            out_sum = partial_sums[1] + jnp.dot(seq_cot.T, attended.reshape(SEQ_LEN, model_width), preferred_element_type=jnp.float32)
            return (qkv_sum, out_sum)

        def inactive_branch(partial_sums):
            return partial_sums
        return (lax.cond(live_flag > 0.5, live_branch, inactive_branch, totals), None)
    start_sums = (jnp.zeros((model_width, 3 * model_width), jnp.float32), jnp.zeros((model_width, model_width), jnp.float32))
    prefix_accumulated = lax.scan(replay_one, start_sums, (logged_seqs, cot_seqs, slot_live))
    qkv_grad, out_grad = prefix_accumulated[0]
    new_qkv, qkv_moment = adam_step(qkv_weight, qkv_first, qkv_second, qkv_grad.reshape(model_width, 3, model_width))
    new_out, out_moment = adam_step(emitted_projection_matrix, out_first, out_second, out_grad)
    fresh_qkv = new_qkv.reshape(model_width, 3 * model_width)

    def recomputed_single(seq_rows):
        projected = jnp.dot(seq_rows, fresh_qkv, preferred_element_type=jnp.float32).reshape(1, SEQ_LEN, 3, model_width)
        attended = attend(projected, decay_mask, norm_gain)[0].reshape(SEQ_LEN, model_width)
        summed = seq_rows.astype(jnp.float32) + jnp.dot(attended, new_out.T, preferred_element_type=jnp.float32)
        return summed.astype(jnp.bfloat16)
    fresh_out = lax.map(recomputed_single, fresh_rows.reshape(-1, SEQ_LEN, model_width)).reshape(-1, model_width)
    return (fresh_out, qkv_moment, out_moment)
```

```python
import functools

import jax
import jax.numpy as jnp
from jax import lax
from jax.experimental import pallas as pl
from jax.experimental.pallas import tpu as pltpu
from jax.sharding import PartitionSpec as P


SEQ_LEN = 256


NORM_FLOOR = 1.0
BETA_ONE = 0.9
BETA_TWO = 0.95
ADAM_EPS = 1e-08
LEARN_RATE = 0.005
WEIGHT_DECAY = 0.1
BIAS_ONE = 0.9999734386011124
BIAS_TWO = 0.994079470779666


def decay_table(decay_logs):
    running = jnp.cumsum(decay_logs, axis=1)
    length = decay_logs.shape[1]
    later = (jnp.arange(length)[:, None] >= jnp.arange(length)[None, :])[None]
    spread_factor = running[:, :, None] - running[:, None, :]
    return jnp.where(later, jnp.exp(jnp.where(later, spread_factor, 0.0)), 0.0)


def multiply(left, right, left_dim, right_dim):
    return lax.dot_general(
        left, right, (((left_dim,), (right_dim,)), ((), ())), preferred_element_type=jnp.float32
    )


def head_forward(raw_query, raw_key, raw_value, mask, gain):
    sigma_query = jax.nn.sigmoid(raw_query)
    sigma_key = jax.nn.sigmoid(raw_key)
    queries = (raw_query * sigma_query).astype(jnp.bfloat16)
    key_rows = (raw_key * sigma_key).astype(jnp.bfloat16)
    values = raw_value.astype(jnp.bfloat16)
    weights = (multiply(queries, key_rows, 1, 1) * mask).astype(jnp.bfloat16)
    mixed = multiply(weights, values, 1, 0)
    mean_square = jnp.mean(mixed * mixed, axis=-1, keepdims=True)
    inverse = lax.rsqrt(jnp.maximum(mean_square, NORM_FLOOR))
    attended = (mixed * inverse * gain).astype(jnp.bfloat16)
    return (
        attended,
        (sigma_query, sigma_key, queries, key_rows, values, weights, mixed, mean_square, inverse),
    )


def adam_step(weight, first_moment, second_moment, gradient):
    first_new = BETA_ONE * first_moment + (1.0 - BETA_ONE) * gradient
    second_new = BETA_TWO * second_moment + (1.0 - BETA_TWO) * gradient * gradient
    update = first_new / BIAS_ONE / (jnp.sqrt(second_new / BIAS_TWO) + ADAM_EPS)
    weight_new = weight - LEARN_RATE * (update + WEIGHT_DECAY * weight)
    return (weight_new.astype(jnp.bfloat16), first_new)


def swap(value, axis, distance):
    count = lax.axis_size(axis)
    return lax.ppermute(value, axis, [(i, i ^ distance) for i in range(count)])


def grouping(count):
    core = 2
    inner = 2
    return count // (core * inner), inner, core


VMEM_LIMIT = 66_000_000
BLOCK_HEADS = 2


def place():
    helper_total = lax.axis_size("helper")
    outer, inner, core = grouping(helper_total)
    helper = lax.axis_index("helper")
    z = helper // (inner * core)
    x = (helper // core) % inner
    c = helper % core

    def at(zz, xx, cc):
        return (zz * inner + xx) * core + cc

    return helper, (outer, inner, core), (z, x, c), at


def remote(source, target, send, recv, peer):
    return pltpu.make_async_remote_copy(
        src_ref=source,
        dst_ref=target,
        send_sem=send,
        recv_sem=recv,
        device_id={"helper": peer},
        device_id_type=pl.DeviceIdType.MESH,
    )


def greet(peers):
    barrier = pltpu.get_barrier_semaphore()
    for peer in peers:
        pl.semaphore_signal(
            barrier, inc=1, device_id={"helper": peer}, device_id_type=pl.DeviceIdType.MESH
        )
    pl.semaphore_wait(barrier, len(peers))


def helper_peers():
    _, (outer, inner, _), (z, x, c), at = place()
    z_peer = [None] + [at((z + k) % outer, x, c) for k in range(1, outer)]
    x_peer = [None] + [at(z, (x + j) % inner, c) for j in range(1, inner)]
    return z_peer, x_peer, at(z, x, 1 - c)


def each(count, body):
    lax.fori_loop(0, count, lambda i, carry: (body(i), carry)[1], 0)


class Gather:
    def __init__(self, steps, piece_at, full, sems):
        self.steps, self.piece_at, self.full = steps, piece_at, full
        self.z_send, self.z_recv, self.x_send, self.x_recv, self.c_send, self.c_recv = sems
        self.helper, (self.outer, self.inner, _), self.spot, self.at = place()
        self.z_peer, self.x_peer, self.c_peer = helper_peers()

    @staticmethod
    def scratch(steps):
        outer, inner, _ = grouping(lax.axis_size("helper"))
        sizes = [outer, outer, inner * outer, inner * outer, inner * outer, inner * outer]
        return [pltpu.SemaphoreType.DMA((steps, size)) for size in sizes]

    def peers(self):
        return self.z_peer[1:] + self.x_peer[1:] + [self.c_peer]

    def owner(self, j, k):
        z, x, c = self.spot
        return self.at((z + self.outer - k) % self.outer, (x + self.inner - j) % self.inner, c)

    def source(self, s, j, k):
        return self.full.at[s, self.owner(j, k)] if j or k else self.piece_at(s)

    def z_copy(self, s, k):
        return remote(
            self.piece_at(s),
            self.full.at[s, self.helper],
            self.z_send.at[s, k],
            self.z_recv.at[s, k],
            self.z_peer[k],
        )

    def x_copy(self, s, j, k):
        slot = j * self.outer + k
        return remote(
            self.source(s, 0, k),
            self.full.at[s, self.owner(0, k)],
            self.x_send.at[s, slot],
            self.x_recv.at[s, slot],
            self.x_peer[j],
        )

    def c_copy(self, s, j, k):
        slot = j * self.outer + k
        return remote(
            self.source(s, j, k),
            self.full.at[s, self.owner(j, k)],
            self.c_send.at[s, slot],
            self.c_recv.at[s, slot],
            self.c_peer,
        )

    lag = 3

    def tick(self, t):
        def stage(s, body):
            pl.when(jnp.logical_and(s >= 0, s < self.steps))(lambda: body(s))

        def begin(s):
            for k in range(1, self.outer):
                self.z_copy(s, k).start()
            for j in range(1, self.inner):
                self.x_copy(s, j, 0).start()
            self.c_copy(s, 0, 0).start()
            self.full[s, self.helper] = self.piece_at(s)[...]

        def after_z(s):
            for k in range(1, self.outer):
                self.z_copy(s, k).wait_recv()
                for j in range(1, self.inner):
                    self.x_copy(s, j, k).start()
                self.c_copy(s, 0, k).start()

        def after_x(s):
            for k in range(self.outer):
                for j in range(1, self.inner):
                    self.x_copy(s, j, k).wait_recv()
                    self.c_copy(s, j, k).start()

        def after_c(s):
            for k in range(self.outer):
                for j in range(self.inner):
                    self.c_copy(s, j, k).wait_recv()

        stage(t, begin)
        stage(t - 1, after_z)
        stage(t - 2, after_x)
        stage(t - 3, after_c)

    def finish(self):
        def drain(s):
            for k in range(self.outer):
                if k:
                    self.z_copy(s, k).wait_send()
                for j in range(self.inner):
                    if j:
                        self.x_copy(s, j, k).wait_send()
                    self.c_copy(s, j, k).wait_send()

        each(self.steps, drain)


def columns(p, width):
    return pl.ds(pl.multiple_of(p * width, width), width)


def head_backward(kept, raw_query, raw_key, cotangent, decay, gain_row):
    sigma_query, sigma_key, queries, key_rows, values, weights, mixed, square, inverse = kept
    active = jnp.where(square > NORM_FLOOR, 1.0, 0.0)
    scaled = cotangent * gain_row
    grad_mixed = inverse * scaled - active * mixed * (inverse * inverse * inverse) * jnp.mean(
        scaled * mixed, axis=-1, keepdims=True
    )
    grad_mixed = grad_mixed.astype(jnp.bfloat16)
    grad_scores = (multiply(grad_mixed, values, 1, 1) * decay).astype(jnp.bfloat16)
    grad_value = multiply(weights, grad_mixed, 0, 0)
    grad_query = multiply(grad_scores, key_rows, 1, 0)
    grad_key = multiply(grad_scores, queries, 0, 0)
    grad_query = grad_query * sigma_query * (1.0 + raw_query * (1.0 - sigma_query))
    grad_key = grad_key * sigma_key * (1.0 + raw_key * (1.0 - sigma_key))
    return grad_query, grad_key, grad_value


def replay_kernel(
    head_width,
    piece,
    logged,
    cotangent,
    mask,
    gain,
    live,
    results,
    turned,
    rows,
    full,
    raw,
    found,
    flipped,
    row_sem,
    found_sem,
    flip_sem,
    *sems,
):
    parts, _, width = piece.shape
    block = full.shape[-1]
    pairs = width // block
    steps = parts * pairs
    capacity = live.shape[0]
    length = mask.shape[1]
    depth = rows.shape[2]
    gather = Gather(steps, lambda s: piece.at[s % parts, :, columns(s // parts, block)], full, sems)
    loads = [
        pltpu.make_async_copy(source, rows.at[i], row_sem.at[i])
        for i, source in enumerate((logged, cotangent))
    ]
    for load in loads:
        load.start()
    greet(gather.peers())

    flips = depth // block

    def flip_copy(i):
        slot = i % 2
        return pltpu.make_async_copy(
            flipped.at[slot],
            turned.at[i // flips, columns(i % flips, block)],
            flip_sem.at[slot],
        )

    def flip(i):
        pl.when(i >= 2)(lambda: flip_copy(i - 2).wait())
        at = columns(i % flips, block)
        for j in range(capacity):
            part = pl.ds(j * length, length)
            flipped[i % 2, :, part] = rows[i // flips, part, at].T
        flip_copy(i).start()

    def found_copy(p, m):
        slot = p % 2
        return pltpu.make_async_copy(
            found.at[slot, m], results.at[m, :, columns(p, block)], found_sem.at[slot, m]
        )

    def heads(p):
        @pl.when(p >= 2)
        def _():
            for m in range(parts):
                found_copy(p - 2, m).wait()

        slot = p % 2

        def one(j):
            part = pl.ds(pl.multiple_of(j * length, length), length)
            alive = live[j] > 0.5
            for n in range(block // head_width):
                at = slice(n * head_width, (n + 1) * head_width)
                decay = mask[p * (block // head_width) + n]
                gain_row = gain[p, :, at]
                raw_query, raw_key = raw[0, part, at], raw[1, part, at]
                attended, kept = head_forward(raw_query, raw_key, raw[2, part, at], decay, gain_row)
                grads = head_backward(
                    kept, raw_query, raw_key, raw[3, part, at], decay, gain_row
                )
                for m, result in enumerate((*grads, attended.astype(jnp.float32))):
                    found[slot, m, part, at] = jnp.where(alive, result, 0.0).astype(jnp.bfloat16)

        each(capacity, one)
        for m in range(parts):
            found_copy(p, m).start()

    def compute(s):
        m = s % parts
        source = jnp.where(m == parts - 1, 1, 0)

        def product(j):
            part = pl.ds(pl.multiple_of(j * length, length), length)
            weight = full[s].reshape(depth, block)
            raw[m, part] = multiply(rows[source, part, :], weight, 1, 0)

        each(capacity, product)
        pl.when(m == parts - 1)(lambda: heads(s // parts))

    def step(t):
        gather.tick(t)

        @pl.when(t == 0)
        def _():
            for load in loads:
                load.wait()

        pl.when(t < 2 * flips)(lambda: flip(t))
        pl.when(t >= gather.lag)(lambda: compute(t - gather.lag))

    each(steps + gather.lag, step)
    for i in range(steps + gather.lag, 2 * flips):
        flip(i)
    for i in range(2 * flips - 2, 2 * flips):
        flip_copy(i).wait()
    for p in range(max(pairs - 2, 0), pairs):
        for m in range(parts):
            found_copy(p, m).wait()
    gather.finish()


def replay(pieces, logged, cotangent, mask, norm_gain, live):
    helper_total = lax.axis_size("helper")
    parts, own, width = pieces.shape
    head_count, length, _ = mask.shape
    head_width = width // head_count
    block = head_width * (BLOCK_HEADS if head_count % BLOCK_HEADS == 0 else 1)
    steps = parts * (width // block)
    row_total, depth = logged.shape
    dma = pltpu.SemaphoreType.DMA
    whole = pl.BlockSpec(memory_space=pltpu.VMEM)
    away = pl.BlockSpec(memory_space=pl.ANY)
    return pl.pallas_call(
        functools.partial(replay_kernel, head_width),
        out_shape=[
            jax.ShapeDtypeStruct((parts, row_total, width), jnp.bfloat16),
            jax.ShapeDtypeStruct((2, depth, row_total), jnp.bfloat16),
        ],
        in_specs=[whole, away, away, whole, whole, whole],
        out_specs=[away, away],
        scratch_shapes=[
            pltpu.VMEM((2, row_total, depth), jnp.bfloat16),
            pltpu.VMEM((steps, helper_total, own, block), jnp.bfloat16),
            pltpu.VMEM((parts, row_total, block), jnp.float32),
            pltpu.VMEM((2, parts, row_total, block), jnp.bfloat16),
            pltpu.VMEM((2, block, row_total), jnp.bfloat16),
            dma((2,)),
            dma((2, parts)),
            dma((2,)),
            *Gather.scratch(steps),
        ],
        compiler_params=pltpu.CompilerParams(
            collective_id=0, has_side_effects=True, vmem_limit_bytes=VMEM_LIMIT
        ),
    )(pieces, logged, cotangent, mask, norm_gain.reshape(-1, 1, block), live)


def reduce_kernel(
    turned,
    results,
    gradient,
    left,
    right,
    own,
    core_out,
    core_in,
    own_x,
    x_out,
    x_in,
    own_z,
    z_out,
    z_in,
    left_sem,
    right_sem,
    c_send,
    c_recv,
    x_send,
    x_recv,
    z_send,
    z_recv,
):
    parts, _, width = results.shape
    block = right.shape[-1]
    pairs = width // block
    steps = parts * pairs
    size = gradient.shape[1]
    _, (outer, inner, core), (z, x, c), _ = place()
    z_peer, x_peer, c_peer = helper_peers()

    def load_right(s):
        return pltpu.make_async_copy(
            results.at[s % parts, :, columns(s // parts, block)], right.at[s], right_sem.at[s]
        )

    def load_left(i):
        return pltpu.make_async_copy(turned.at[i], left.at[i], left_sem.at[i])

    load_left(0).start()
    load_right(0).start()
    for s in range(1, parts):
        load_right(s).start()
    load_left(1).start()
    for s in range(parts, steps):
        load_right(s).start()
    greet(z_peer[1:] + x_peer[1:] + [c_peer])

    def c_copy(s):
        return remote(core_out.at[s % 2], core_in.at[s], c_send.at[s], c_recv.at[s], c_peer)

    def x_copy(s, j):
        return remote(
            x_out.at[s % 2, j], x_in.at[s, j], x_send.at[s, j], x_recv.at[s, j], x_peer[j]
        )

    def z_copy(s, k):
        return remote(
            z_out.at[s % 2, k], z_in.at[s, k], z_send.at[s, k], z_recv.at[s, k], z_peer[k]
        )

    def begin(s):
        load_right(s).wait()
        pl.when(s == 0)(lambda: load_left(0).wait())
        pl.when(s == parts - 1)(lambda: load_left(1).wait())
        pl.when(s >= 2)(lambda: c_copy(s - 2).wait_send())
        source = jnp.where(s % parts == parts - 1, 1, 0)
        slot = s % 2

        def one(q):
            span = core * size
            part = pl.ds(pl.multiple_of(q * span, span), span)
            total = multiply(left[source, part, :], right[s], 1, 0)
            first, second = total[:size], total[size:]
            own[slot, q] = jnp.where(c == 0, first, second)
            core_out[slot, q] = jnp.where(c == 0, second, first).astype(jnp.bfloat16)

        each(outer * inner, one)
        c_copy(s).start()

    def after_c(s):
        c_copy(s).wait_recv()
        slot = s % 2

        @pl.when(s >= 2)
        def _():
            for j in range(1, inner):
                x_copy(s - 2, j).wait_send()

        for j in range(1, inner):
            for k in range(outer):
                q = k * inner + (x + j) % inner
                x_out[slot, j, k] = (own[slot, q] + core_in[s, q]).astype(jnp.bfloat16)
            x_copy(s, j).start()
        for k in range(outer):
            q = k * inner + x
            own_x[slot, k] = own[slot, q] + core_in[s, q]

    def after_x(s):
        slot = s % 2
        for j in range(1, inner):
            x_copy(s, j).wait_recv()

        @pl.when(s >= 2)
        def _():
            for k in range(1, outer):
                z_copy(s - 2, k).wait_send()

        def total(q):
            value = own_x[slot, q]
            for j in range(1, inner):
                value = value + x_in[s, j, q]
            return value

        for k in range(1, outer):
            z_out[slot, k] = total((z + k) % outer).astype(jnp.bfloat16)
            z_copy(s, k).start()
        own_z[slot] = total(z)

    def after_z(s):
        value = own_z[s % 2]
        for k in range(1, outer):
            z_copy(s, k).wait_recv()
            value = value + z_in[s, k]
        gradient[s % parts, :, columns(s // parts, block)] = value

    def step(t):
        for lag, body in enumerate((begin, after_c, after_x, after_z)):
            s = t - lag
            pl.when(jnp.logical_and(s >= 0, s < steps))(functools.partial(body, s))

    each(steps + 3, step)
    for s in range(max(steps - 2, 0), steps):
        c_copy(s).wait_send()
        for j in range(1, inner):
            x_copy(s, j).wait_send()
        for k in range(1, outer):
            z_copy(s, k).wait_send()


def reduce_gradients(turned, results, head_count):
    helper_total = lax.axis_size("helper")
    outer, inner, core = grouping(helper_total)
    parts, row_total, width = results.shape
    depth = turned.shape[1]
    size = depth // helper_total
    block = width // head_count * (BLOCK_HEADS if head_count % BLOCK_HEADS == 0 else 1)
    steps = parts * (width // block)
    dma = pltpu.SemaphoreType.DMA
    half, full = jnp.bfloat16, jnp.float32
    tile = (size, block)
    away = pl.BlockSpec(memory_space=pl.ANY)
    return pl.pallas_call(
        reduce_kernel,
        out_shape=jax.ShapeDtypeStruct((parts, size, width), full),
        in_specs=[away, away],
        out_specs=pl.BlockSpec(memory_space=pltpu.VMEM),
        scratch_shapes=[
            pltpu.VMEM((2, depth, row_total), half),
            pltpu.VMEM((steps, row_total, block), half),
            pltpu.VMEM((2, outer * inner, *tile), full),
            pltpu.VMEM((2, outer * inner, *tile), half),
            pltpu.VMEM((steps, outer * inner, *tile), half),
            pltpu.VMEM((2, outer, *tile), full),
            pltpu.VMEM((2, inner, outer, *tile), half),
            pltpu.VMEM((steps, inner, outer, *tile), half),
            pltpu.VMEM((2, *tile), full),
            pltpu.VMEM((2, outer, *tile), half),
            pltpu.VMEM((steps, outer, *tile), half),
            dma((2,)),
            dma((steps,)),
            dma((steps,)),
            dma((steps,)),
            dma((steps, inner)),
            dma((steps, inner)),
            dma((steps, outer)),
            dma((steps, outer)),
        ],
        compiler_params=pltpu.CompilerParams(
            collective_id=1, has_side_effects=True, vmem_limit_bytes=VMEM_LIMIT
        ),
    )(turned, results)


def fresh_kernel(head_width, piece, fresh, mask, gain, out, full, raw, *sems):
    parts, _, width = piece.shape
    block = full.shape[-1]
    pairs = width // block
    steps = parts * pairs
    depth = fresh.shape[1]
    gather = Gather(
        steps,
        lambda s: piece.at[(s + parts - 1) % parts, :, columns(s // parts, block)],
        full,
        sems,
    )
    greet(gather.peers())
    out[...] = jnp.zeros_like(out)

    def heads(p):
        attended = []
        for n in range(block // head_width):
            at = slice(n * head_width, (n + 1) * head_width)
            decay = mask[p * (block // head_width) + n]
            attended.append(
                head_forward(raw[0, :, at], raw[1, :, at], raw[2, :, at], decay, gain[p, :, at])[0]
            )
        attended = jnp.concatenate(attended, axis=1)
        weight = full[p * parts].reshape(depth, block)
        out[...] += multiply(attended, weight, 1, 1)

    def compute(s):
        m = s % parts

        @pl.when(m > 0)
        def _():
            raw[m - 1] = multiply(fresh[...], full[s].reshape(depth, block), 1, 0)

        pl.when(m == parts - 1)(lambda: heads(s // parts))

    def step(t):
        gather.tick(t)
        pl.when(t >= gather.lag)(lambda: compute(t - gather.lag))

    each(steps + gather.lag, step)
    gather.finish()


def fresh_forward(pieces, fresh, mask, norm_gain):
    helper_total = lax.axis_size("helper")
    parts, own, width = pieces.shape
    head_count = mask.shape[0]
    head_width = width // head_count
    block = head_width * (BLOCK_HEADS if head_count % BLOCK_HEADS == 0 else 1)
    steps = parts * (width // block)
    row_total, depth = fresh.shape
    whole = pl.BlockSpec(memory_space=pltpu.VMEM)
    return pl.pallas_call(
        functools.partial(fresh_kernel, head_width),
        out_shape=jax.ShapeDtypeStruct((row_total, own * helper_total), jnp.float32),
        in_specs=[whole] * 4,
        out_specs=whole,
        scratch_shapes=[
            pltpu.VMEM((steps, helper_total, own, block), jnp.bfloat16),
            pltpu.VMEM((parts - 1, row_total, block), jnp.float32),
            *Gather.scratch(steps),
        ],
        compiler_params=pltpu.CompilerParams(
            collective_id=2, has_side_effects=True, vmem_limit_bytes=VMEM_LIMIT
        ),
    )(pieces, fresh, mask, norm_gain.reshape(-1, 1, block))


def local(
    recorded_input_rows,
    out_cotangent,
    fresh_rows,
    seq_counts,
    decay_logs,
    norm_gain,
    qkv_weight,
    emitted_projection_matrix,
    qkv_first,
    qkv_second,
    out_first,
    out_second,
):
    helper_total = lax.axis_size("helper")
    helper = lax.axis_index("helper")
    head_count = decay_logs.shape[0]
    weights = [qkv_weight[:, m] for m in range(3)] + [emitted_projection_matrix]
    old = jnp.stack([weight.astype(jnp.bfloat16) for weight in weights])
    decay_mask = decay_table(decay_logs)
    own_count = jnp.sum(jnp.where(jnp.arange(helper_total) == helper, seq_counts, 0))
    capacity = recorded_input_rows.shape[0] // SEQ_LEN
    live = (jnp.arange(capacity) < own_count).astype(jnp.float32)
    live = jnp.broadcast_to(live[:, None, None], (capacity, 1, qkv_weight.shape[2] // head_count))

    results, turned = replay(
        old, recorded_input_rows, out_cotangent, decay_mask, norm_gain, live
    )
    gradient = reduce_gradients(turned, results, head_count)
    pieces, moments = [], []
    for m in range(3):
        piece, moment = adam_step(
            qkv_weight[:, m], qkv_first[:, m], qkv_second[:, m], gradient[m]
        )
        pieces.append(piece)
        moments.append(moment)
    new_out, out_moment = adam_step(emitted_projection_matrix, out_first, out_second, gradient[3])
    qkv_moment = jnp.stack(moments, axis=1)
    new = jnp.stack(pieces + [new_out])
    partial_out = fresh_forward(new, fresh_rows, decay_mask, norm_gain)
    fresh_out = finish(partial_out, fresh_rows)
    return (fresh_out, qkv_moment, out_moment)


def finish(partial_out, fresh):
    if lax.axis_size("tensor") == 2:
        width = partial_out.shape[1] // 2
        first = lax.axis_index("tensor") == 0
        left, right = partial_out[:, :width], partial_out[:, width:]
        came = swap(jnp.where(first, right, left).astype(jnp.bfloat16), "tensor", 1)
        residual = jnp.where(first, fresh[:, :width], fresh[:, width:])
        piece = residual.astype(jnp.float32) + (jnp.where(first, left, right) + came)
        piece = piece.astype(jnp.bfloat16)
        other = swap(piece, "tensor", 1)
        return jnp.concatenate(
            [jnp.where(first, piece, other), jnp.where(first, other, piece)], axis=1
        )
    share_sum = lax.psum_scatter(partial_out, "tensor", scatter_dimension=1, tiled=True)
    width = share_sum.shape[1]
    residual = lax.dynamic_slice_in_dim(fresh, lax.axis_index("tensor") * width, width, 1)
    piece = (residual.astype(jnp.float32) + share_sum).astype(jnp.bfloat16)
    return lax.all_gather(piece, "tensor", axis=1, tiled=True)


def solution(mesh):
    return jax.shard_map(
        local,
        mesh=mesh,
        in_specs=(
            P("helper", None),
            P("helper", None),
            P("helper", None),
            P(),
            P("tensor", None),
            P("tensor"),
            P("helper", None, "tensor"),
            P("helper", "tensor"),
            P("helper", None, "tensor"),
            P("helper", None, "tensor"),
            P("helper", "tensor"),
            P("helper", "tensor"),
        ),
        out_specs=(P("helper", None), P("helper", None, "tensor"), P("helper", "tensor")),
        check_vma=False,
    )
```

```python
import functools

import jax
import jax.numpy as jnp
from jax import lax
from jax.experimental import pallas as pl
from jax.experimental.pallas import tpu as pltpu
from jax.sharding import PartitionSpec as P


SEQ_LEN = 256


NORM_FLOOR = 1.0
BETA_ONE = 0.9
BETA_TWO = 0.95
ADAM_EPS = 1e-08
LEARN_RATE = 0.005
WEIGHT_DECAY = 0.1
BIAS_ONE = 0.9999734386011124
BIAS_TWO = 0.994079470779666


def multiply(left, right, left_dim, right_dim):
    return lax.dot_general(
        left, right, (((left_dim,), (right_dim,)), ((), ())), preferred_element_type=jnp.float32
    )


def head_forward(raw_query, raw_key, raw_value, mask, gain):
    sigma_query = jax.nn.sigmoid(raw_query)
    sigma_key = jax.nn.sigmoid(raw_key)
    queries = (raw_query * sigma_query).astype(jnp.bfloat16)
    key_rows = (raw_key * sigma_key).astype(jnp.bfloat16)
    values = raw_value.astype(jnp.bfloat16)
    weights = (multiply(queries, key_rows, 1, 1) * mask).astype(jnp.bfloat16)
    mixed = multiply(weights, values, 1, 0)
    mean_square = jnp.mean(mixed * mixed, axis=-1, keepdims=True)
    inverse = lax.rsqrt(jnp.maximum(mean_square, NORM_FLOOR))
    attended = (mixed * inverse * gain).astype(jnp.bfloat16)
    return (
        attended,
        (sigma_query, sigma_key, queries, key_rows, values, weights, mixed, mean_square, inverse),
    )


def adam_step(weight, first_moment, second_moment, gradient):
    first_new = BETA_ONE * first_moment + (1.0 - BETA_ONE) * gradient
    second_new = BETA_TWO * second_moment + (1.0 - BETA_TWO) * gradient * gradient
    update = first_new / BIAS_ONE / (jnp.sqrt(second_new / BIAS_TWO) + ADAM_EPS)
    weight_new = weight - LEARN_RATE * (update + WEIGHT_DECAY * weight)
    return (weight_new.astype(jnp.bfloat16), first_new)


def swap(value, axis, distance):
    count = lax.axis_size(axis)
    return lax.ppermute(value, axis, [(i, i ^ distance) for i in range(count)])


def grouping(count):
    core = 2
    inner = 2
    return count // (core * inner), inner, core


VMEM_LIMIT = 66_000_000
BLOCK_HEADS = 2


def place():
    helper_total = lax.axis_size("helper")
    outer, inner, core = grouping(helper_total)
    helper = lax.axis_index("helper")
    z = helper // (inner * core)
    x = (helper // core) % inner
    c = helper % core

    def at(zz, xx, cc):
        return (zz * inner + xx) * core + cc

    return helper, (outer, inner, core), (z, x, c), at


def remote(source, target, send, recv, peer, axis="helper"):
    return pltpu.make_async_remote_copy(
        src_ref=source,
        dst_ref=target,
        send_sem=send,
        recv_sem=recv,
        device_id={axis: peer},
        device_id_type=pl.DeviceIdType.MESH,
    )


def greet(peers, across=False):
    barrier = pltpu.get_barrier_semaphore()
    targets = [{"helper": peer} for peer in peers]
    if across:
        targets.append({"tensor": 1 - lax.axis_index("tensor")})
    for target in targets:
        pl.semaphore_signal(
            barrier, inc=1, device_id=target, device_id_type=pl.DeviceIdType.MESH
        )
    pl.semaphore_wait(barrier, len(targets))


def helper_peers():
    _, (outer, inner, _), (z, x, c), at = place()
    z_peer = [None] + [at((z + k) % outer, x, c) for k in range(1, outer)]
    x_peer = [None] + [at(z, (x + j) % inner, c) for j in range(1, inner)]
    return z_peer, x_peer, at(z, x, 1 - c)


def each(count, body):
    lax.fori_loop(0, count, lambda i, carry: (body(i), carry)[1], 0)


class Gather:
    def __init__(self, steps, piece_at, full, sems):
        self.steps, self.piece_at, self.full = steps, piece_at, full
        self.z_send, self.z_recv, self.x_send, self.x_recv, self.c_send, self.c_recv = sems
        self.helper, (self.outer, self.inner, _), self.spot, self.at = place()
        self.z_peer, self.x_peer, self.c_peer = helper_peers()

    @staticmethod
    def scratch(steps):
        outer, inner, _ = grouping(lax.axis_size("helper"))
        sizes = [outer, outer, inner * outer, inner * outer, inner * outer, inner * outer]
        return [pltpu.SemaphoreType.DMA((steps, size)) for size in sizes]

    def peers(self):
        return self.z_peer[1:] + self.x_peer[1:] + [self.c_peer]

    def owner(self, j, k):
        z, x, c = self.spot
        return self.at((z + self.outer - k) % self.outer, (x + self.inner - j) % self.inner, c)

    def source(self, s, j, k):
        return self.full.at[s, self.owner(j, k)] if j or k else self.piece_at(s)

    def z_copy(self, s, k):
        return remote(
            self.piece_at(s),
            self.full.at[s, self.helper],
            self.z_send.at[s, k],
            self.z_recv.at[s, k],
            self.z_peer[k],
        )

    def x_copy(self, s, j, k):
        slot = j * self.outer + k
        return remote(
            self.source(s, 0, k),
            self.full.at[s, self.owner(0, k)],
            self.x_send.at[s, slot],
            self.x_recv.at[s, slot],
            self.x_peer[j],
        )

    def c_copy(self, s, j, k):
        slot = j * self.outer + k
        return remote(
            self.source(s, j, k),
            self.full.at[s, self.owner(j, k)],
            self.c_send.at[s, slot],
            self.c_recv.at[s, slot],
            self.c_peer,
        )

    lag = 2

    def stage(self, s, body):
        pl.when(jnp.logical_and(s >= 0, s < self.steps))(lambda: body(s))

    def begin(self, s):
        for k in range(1, self.outer):
            self.z_copy(s, k).start()
        for j in range(1, self.inner):
            self.x_copy(s, j, 0).start()
        self.c_copy(s, 0, 0).start()
        self.full[s, self.helper] = self.piece_at(s)[...]

    def after_z(self, s):
        for k in range(1, self.outer):
            self.z_copy(s, k).wait_recv()
            for j in range(1, self.inner):
                self.x_copy(s, j, k).start()
            self.c_copy(s, 0, k).start()

    def after_x(self, s):
        for k in range(self.outer):
            for j in range(1, self.inner):
                self.x_copy(s, j, k).wait_recv()
                self.c_copy(s, j, k).start()

    def after_c(self, s):
        for k in range(self.outer):
            for j in range(self.inner):
                self.c_copy(s, j, k).wait_recv()

    def tick(self, t):
        self.stage(t + 1, self.begin)
        self.stage(t - 1, self.after_z)
        self.stage(t - 2, self.after_x)

    def finish(self):
        def drain(s):
            for k in range(self.outer):
                if k:
                    self.z_copy(s, k).wait_send()
                for j in range(self.inner):
                    if j:
                        self.x_copy(s, j, k).wait_send()
                    self.c_copy(s, j, k).wait_send()

        each(self.steps, drain)


def columns(p, width):
    return pl.ds(pl.multiple_of(p * width, width), width)


def fill_mask(mask, across, down):
    length = mask.shape[1]
    later = lax.broadcasted_iota(jnp.int32, (length, length), 0) >= lax.broadcasted_iota(
        jnp.int32, (length, length), 1
    )
    for n in range(mask.shape[0]):
        spread_factor = down[:, n : n + 1] - across[n : n + 1, :]
        mask[n] = jnp.where(later, jnp.exp(jnp.where(later, spread_factor, 0.0)), 0.0)


def head_backward(kept, raw_query, raw_key, cotangent, decay, gain_row):
    sigma_query, sigma_key, queries, key_rows, values, weights, mixed, square, inverse = kept
    active = jnp.where(square > NORM_FLOOR, 1.0, 0.0)
    scaled = cotangent * gain_row
    grad_mixed = inverse * scaled - active * mixed * (inverse * inverse * inverse) * jnp.mean(
        scaled * mixed, axis=-1, keepdims=True
    )
    grad_mixed = grad_mixed.astype(jnp.bfloat16)
    grad_scores = (multiply(grad_mixed, values, 1, 1) * decay).astype(jnp.bfloat16)
    grad_value = multiply(weights, grad_mixed, 0, 0)
    grad_query = multiply(grad_scores, key_rows, 1, 0)
    grad_key = multiply(grad_scores, queries, 0, 0)
    grad_query = grad_query * sigma_query * (1.0 + raw_query * (1.0 - sigma_query))
    grad_key = grad_key * sigma_key * (1.0 + raw_key * (1.0 - sigma_key))
    return grad_query, grad_key, grad_value


def replay_kernel(
    head_width,
    qkv_weight,
    out_weight,
    logged,
    cotangent,
    across,
    down,
    gain,
    live,
    results,
    turned,
    piece,
    mask,
    rows,
    full,
    raw,
    found,
    flipped,
    row_sem,
    found_sem,
    flip_sem,
    *sems,
):
    parts, _, width = piece.shape
    block = full.shape[-1]
    pairs = width // block
    steps = parts * pairs
    capacity = live.shape[0]
    length = mask.shape[1]
    depth = rows.shape[2]
    gather = Gather(steps, lambda s: piece.at[s % parts, :, columns(s // parts, block)], full, sems)
    loads = [
        pltpu.make_async_copy(source, rows.at[i], row_sem.at[i])
        for i, source in enumerate((logged, cotangent))
    ]
    for load in loads:
        load.start()
    for m in range(parts - 1):
        piece[m] = qkv_weight[m].astype(jnp.bfloat16)
    piece[parts - 1] = out_weight[...].astype(jnp.bfloat16)
    greet(gather.peers())
    gather.begin(0)
    gather.stage(1, gather.begin)
    fill_mask(mask, across, down)
    for load in loads:
        load.wait()

    flips = depth // block
    flip_ticks = 4
    flip_share = -(-2 * flips // flip_ticks)

    def flip_copy(i):
        slot = i % 2
        return pltpu.make_async_copy(
            flipped.at[slot],
            turned.at[i // flips, columns(i % flips, block)],
            flip_sem.at[slot],
        )

    def flip(i):
        pl.when(i >= 2)(lambda: flip_copy(i - 2).wait())
        at = columns(i % flips, block)
        for j in range(capacity):
            part = pl.ds(j * length, length)
            flipped[i % 2, :, part] = rows[i // flips, part, at].T
        flip_copy(i).start()

    def found_copy(p, m):
        slot = p % 2
        return pltpu.make_async_copy(
            found.at[slot, m], results.at[m, :, columns(p, block)], found_sem.at[slot, m]
        )

    share = -(-capacity // parts)

    def heads(p, m):
        slot = p % 2

        @pl.when(jnp.logical_and(m == 0, p >= 2))
        def _():
            for i in range(parts):
                found_copy(p - 2, i).wait()

        def one(j):
            part = pl.ds(pl.multiple_of(j * length, length), length)
            alive = live[j] > 0.5
            for n in range(block // head_width):
                at = slice(n * head_width, (n + 1) * head_width)
                decay = mask[p * (block // head_width) + n]
                gain_row = gain[p, :, at]
                raw_query, raw_key = raw[slot, 0, part, at], raw[slot, 1, part, at]
                attended, kept = head_forward(
                    raw_query, raw_key, raw[slot, 2, part, at], decay, gain_row
                )
                grads = head_backward(
                    kept, raw_query, raw_key, raw[slot, 3, part, at], decay, gain_row
                )
                for i, result in enumerate((*grads, attended.astype(jnp.float32))):
                    found[slot, i, part, at] = jnp.where(alive, result, 0.0).astype(jnp.bfloat16)

        for i in range(share):
            j = m * share + i
            pl.when(j < capacity)(functools.partial(one, j))

        @pl.when(m == parts - 1)
        def _():
            for i in range(parts):
                found_copy(p, i).start()

    def product(s):
        m = s % parts
        p = s // parts
        source = jnp.where(m == parts - 1, 1, 0)

        def one(j):
            part = pl.ds(pl.multiple_of(j * length, length), length)
            weight = full[s].reshape(depth, block)
            raw[p % 2, m, part] = multiply(rows[source, part, :], weight, 1, 0)

        each(capacity, one)

    def step(t):
        pl.when(t > 0)(lambda: gather.tick(t))

        @pl.when(t < flip_ticks)
        def _():
            for i in range(flip_share):
                pl.when(t * flip_share + i < 2 * flips)(lambda i=i: flip(t * flip_share + i))

        s = t - gather.lag
        pl.when(s >= parts)(lambda: heads(s // parts - 1, s % parts))

        @pl.when(jnp.logical_and(s >= 0, s < steps))
        def _():
            gather.after_c(s)
            product(s)

    each(steps + parts + gather.lag, step)
    for i in range(2 * flips - 2, 2 * flips):
        flip_copy(i).wait()
    for p in range(max(pairs - 2, 0), pairs):
        for m in range(parts):
            found_copy(p, m).wait()
    gather.finish()


def replay(qkv_weight, out_weight, logged, cotangent, running, norm_gain, live):
    helper_total = lax.axis_size("helper")
    parts, own, width = qkv_weight.shape[0] + 1, *out_weight.shape
    head_count, length = running.shape
    head_width = width // head_count
    block = head_width * (BLOCK_HEADS if head_count % BLOCK_HEADS == 0 else 1)
    steps = parts * (width // block)
    row_total, depth = logged.shape
    dma = pltpu.SemaphoreType.DMA
    whole = pl.BlockSpec(memory_space=pltpu.VMEM)
    away = pl.BlockSpec(memory_space=pl.ANY)
    return pl.pallas_call(
        functools.partial(replay_kernel, head_width),
        out_shape=[
            jax.ShapeDtypeStruct((parts, row_total, width), jnp.bfloat16),
            jax.ShapeDtypeStruct((2, depth, row_total), jnp.bfloat16),
        ],
        in_specs=[whole, whole, away, away, whole, whole, whole, whole],
        out_specs=[away, away],
        scratch_shapes=[
            pltpu.VMEM((parts, own, width), jnp.bfloat16),
            pltpu.VMEM((head_count, length, length), jnp.float32),
            pltpu.VMEM((2, row_total, depth), jnp.bfloat16),
            pltpu.VMEM((steps, helper_total, own, block), jnp.bfloat16),
            pltpu.VMEM((2, parts, row_total, block), jnp.float32),
            pltpu.VMEM((2, parts, row_total, block), jnp.bfloat16),
            pltpu.VMEM((2, block, row_total), jnp.bfloat16),
            dma((2,)),
            dma((2, parts)),
            dma((2,)),
            *Gather.scratch(steps),
        ],
        compiler_params=pltpu.CompilerParams(
            collective_id=0, has_side_effects=True, vmem_limit_bytes=VMEM_LIMIT
        ),
    )(
        qkv_weight,
        out_weight,
        logged,
        cotangent,
        running,
        running.T,
        norm_gain.reshape(-1, 1, block),
        live,
    )


def reduce_kernel(
    turned,
    results,
    qkv_weight,
    out_weight,
    qkv_first,
    out_first,
    qkv_second,
    out_second,
    pieces,
    qkv_moment,
    out_moment,
    left,
    right,
    own,
    core_out,
    core_in,
    own_x,
    x_out,
    x_in,
    own_z,
    z_out,
    z_in,
    left_sem,
    right_sem,
    c_send,
    c_recv,
    x_send,
    x_recv,
    z_send,
    z_recv,
):
    parts, _, width = results.shape
    block = right.shape[-1]
    pairs = width // block
    steps = parts * pairs
    size = out_weight.shape[0]
    _, (outer, inner, core), (z, x, c), _ = place()
    z_peer, x_peer, c_peer = helper_peers()

    def load_right(s):
        return pltpu.make_async_copy(
            results.at[s % parts, :, columns(s // parts, block)], right.at[s], right_sem.at[s]
        )

    def load_left(i):
        return pltpu.make_async_copy(turned.at[i], left.at[i], left_sem.at[i])

    load_left(0).start()
    load_right(0).start()
    for s in range(1, parts):
        load_right(s).start()
    load_left(1).start()
    for s in range(parts, steps):
        load_right(s).start()
    greet(z_peer[1:] + x_peer[1:] + [c_peer])

    def c_copy(s):
        return remote(core_out.at[s % 2], core_in.at[s], c_send.at[s], c_recv.at[s], c_peer)

    def x_copy(s, j):
        return remote(
            x_out.at[s % 2, j], x_in.at[s, j], x_send.at[s, j], x_recv.at[s, j], x_peer[j]
        )

    def z_copy(s, k):
        return remote(
            z_out.at[s % 2, k], z_in.at[s, k], z_send.at[s, k], z_recv.at[s, k], z_peer[k]
        )

    def begin(s):
        load_right(s).wait()
        pl.when(s == 0)(lambda: load_left(0).wait())
        pl.when(s == parts - 1)(lambda: load_left(1).wait())
        pl.when(s >= 2)(lambda: c_copy(s - 2).wait_send())
        source = jnp.where(s % parts == parts - 1, 1, 0)
        slot = s % 2

        def one(q):
            span = core * size
            part = pl.ds(pl.multiple_of(q * span, span), span)
            total = multiply(left[source, part, :], right[s], 1, 0)
            first, second = total[:size], total[size:]
            own[slot, q] = jnp.where(c == 0, first, second)
            core_out[slot, q] = jnp.where(c == 0, second, first).astype(jnp.bfloat16)

        each(outer * inner, one)
        c_copy(s).start()

    def after_c(s):
        c_copy(s).wait_recv()
        slot = s % 2

        @pl.when(s >= 2)
        def _():
            for j in range(1, inner):
                x_copy(s - 2, j).wait_send()

        for j in range(1, inner):
            for k in range(outer):
                q = k * inner + (x + j) % inner
                x_out[slot, j, k] = (own[slot, q] + core_in[s, q]).astype(jnp.bfloat16)
            x_copy(s, j).start()
        for k in range(outer):
            q = k * inner + x
            own_x[slot, k] = own[slot, q] + core_in[s, q]

    def after_x(s):
        slot = s % 2
        for j in range(1, inner):
            x_copy(s, j).wait_recv()

        @pl.when(s >= 2)
        def _():
            for k in range(1, outer):
                z_copy(s - 2, k).wait_send()

        def total(q):
            value = own_x[slot, q]
            for j in range(1, inner):
                value = value + x_in[s, j, q]
            return value

        for k in range(1, outer):
            z_out[slot, k] = total((z + k) % outer).astype(jnp.bfloat16)
            z_copy(s, k).start()
        own_z[slot] = total(z)

    def after_z(s):
        value = own_z[s % 2]
        for k in range(1, outer):
            z_copy(s, k).wait_recv()
            value = value + z_in[s, k]
        m = s % parts
        at = columns(s // parts, block)

        @pl.when(m < parts - 1)
        def _():
            piece, moment = adam_step(
                qkv_weight[m, :, at], qkv_first[m, :, at], qkv_second[m, :, at], value
            )
            pieces[m, :, at] = piece
            qkv_moment[m, :, at] = moment

        @pl.when(m == parts - 1)
        def _():
            piece, moment = adam_step(
                out_weight[:, at], out_first[:, at], out_second[:, at], value
            )
            pieces[m, :, at] = piece
            out_moment[:, at] = moment

    def step(t):
        for lag, body in enumerate((begin, after_c, after_x, after_z)):
            s = t - lag
            pl.when(jnp.logical_and(s >= 0, s < steps))(functools.partial(body, s))

    each(steps + 3, step)
    for s in range(max(steps - 2, 0), steps):
        c_copy(s).wait_send()
        for j in range(1, inner):
            x_copy(s, j).wait_send()
        for k in range(1, outer):
            z_copy(s, k).wait_send()


def reduce_gradients(turned, results, states, head_count):
    helper_total = lax.axis_size("helper")
    outer, inner, core = grouping(helper_total)
    parts, row_total, width = results.shape
    depth = turned.shape[1]
    size = depth // helper_total
    block = width // head_count * (BLOCK_HEADS if head_count % BLOCK_HEADS == 0 else 1)
    steps = parts * (width // block)
    dma = pltpu.SemaphoreType.DMA
    half, full = jnp.bfloat16, jnp.float32
    tile = (size, block)
    whole = pl.BlockSpec(memory_space=pltpu.VMEM)
    away = pl.BlockSpec(memory_space=pl.ANY)
    return pl.pallas_call(
        reduce_kernel,
        out_shape=[
            jax.ShapeDtypeStruct((parts, size, width), half),
            jax.ShapeDtypeStruct((parts - 1, size, width), full),
            jax.ShapeDtypeStruct((size, width), full),
        ],
        in_specs=[away, away] + [whole] * 6,
        out_specs=[whole] * 3,
        scratch_shapes=[
            pltpu.VMEM((2, depth, row_total), half),
            pltpu.VMEM((steps, row_total, block), half),
            pltpu.VMEM((2, outer * inner, *tile), full),
            pltpu.VMEM((2, outer * inner, *tile), half),
            pltpu.VMEM((steps, outer * inner, *tile), half),
            pltpu.VMEM((2, outer, *tile), full),
            pltpu.VMEM((2, inner, outer, *tile), half),
            pltpu.VMEM((steps, inner, outer, *tile), half),
            pltpu.VMEM((2, *tile), full),
            pltpu.VMEM((2, outer, *tile), half),
            pltpu.VMEM((steps, outer, *tile), half),
            dma((2,)),
            dma((steps,)),
            dma((steps,)),
            dma((steps,)),
            dma((steps, inner)),
            dma((steps, inner)),
            dma((steps, outer)),
            dma((steps, outer)),
        ],
        compiler_params=pltpu.CompilerParams(
            collective_id=1, has_side_effects=True, vmem_limit_bytes=VMEM_LIMIT
        ),
    )(turned, results, *states)


def fresh_kernel(head_width, piece, fresh, across, down, gain, out, *scratch):
    exchange = out.dtype == fresh.dtype
    full, raw, mask, attended, total = scratch[:5]
    sems = scratch[5:]
    if exchange:
        other, other_attended, other_total, *marks = scratch[5:14]
        sems = scratch[14:]
    parts, _, width = piece.shape
    block = full.shape[-1]
    pairs = width // block
    steps = parts * pairs
    depth = fresh.shape[1]

    def piece_at(s):
        later = s - pairs
        m = jnp.where(later < 0, parts - 1, later % (parts - 1))
        p = jnp.where(later < 0, s, later // (parts - 1))
        return piece.at[m, :, columns(p, block)]

    gather = Gather(steps, piece_at, full, sems)
    greet(gather.peers(), exchange)
    gather.begin(0)
    gather.stage(1, gather.begin)
    fill_mask(mask, across, down)
    total[...] = jnp.zeros_like(total)
    if exchange:
        other_total[...] = jnp.zeros_like(other_total)
        partner = 1 - lax.axis_index("tensor")
        y_send, y_recv, c_send, c_recv, a_send, a_recv = marks
        share = full.shape[1] // 2
        half = pl.ds(pl.multiple_of(gather.spot[2] * share, share), share)

        def y_copy(p):
            return remote(
                full.at[p, half], other.at[p, half], y_send.at[p], y_recv.at[p], partner, "tensor"
            )

        def c_copy(p):
            return remote(
                other.at[p, half], other.at[p, half], c_send.at[p], c_recv.at[p], gather.c_peer
            )

        def a_copy(p):
            return remote(
                attended.at[p], other_attended.at[p], a_send.at[p], a_recv.at[p], partner, "tensor"
            )

        def take_other(p):
            a_copy(p).wait_recv()
            c_copy(p).wait_recv()
            weight = other[p].reshape(depth, block)
            other_total[...] += multiply(other_attended[p], weight, 1, 1)

        def relay(i):
            y_copy(i).wait_recv()
            c_copy(i).start()

    def heads(p):
        for n in range(block // head_width):
            at = slice(n * head_width, (n + 1) * head_width)
            decay = mask[p * (block // head_width) + n]
            attended[p, :, at] = head_forward(
                raw[0, :, at], raw[1, :, at], raw[2, :, at], decay, gain[p, :, at]
            )[0]
        if exchange:
            a_copy(p).start()
        total[...] += multiply(attended[p], full[p].reshape(depth, block), 1, 1)
        if exchange:
            pl.when(p > 0)(lambda: take_other(p - 1))

    def compute(s):
        gather.after_c(s)
        if exchange:
            pl.when(s < pairs)(lambda: y_copy(s).start())
            since = s - 3
            turn = jnp.logical_and(since >= 0, since < 2 * pairs)
            pl.when(jnp.logical_and(turn, since % 2 == 0))(lambda: relay(since // 2))

        @pl.when(s >= pairs)
        def _():
            m = (s - pairs) % (parts - 1)
            raw[m] = multiply(fresh[...], full[s].reshape(depth, block), 1, 0)
            pl.when(m == parts - 2)(lambda: heads((s - pairs) // (parts - 1)))

    def step(t):
        pl.when(t > 0)(lambda: gather.tick(t))
        pl.when(t >= gather.lag)(lambda: compute(t - gather.lag))

    each(steps + gather.lag, step)
    if exchange:
        for p in range(pairs):
            if 3 + 2 * p >= steps:
                relay(p)
        take_other(pairs - 1)
        summed = total[...] + other_total[...]
        out[...] = (fresh[...].astype(jnp.float32) + summed).astype(out.dtype)
        for p in range(pairs):
            y_copy(p).wait_send()
            c_copy(p).wait_send()
            a_copy(p).wait_send()
    else:
        out[...] = total[...]
    gather.finish()


def fresh_forward(pieces, fresh, running, norm_gain):
    helper_total = lax.axis_size("helper")
    exchange = lax.axis_size("tensor") == 2
    parts, own, width = pieces.shape
    head_count, length = running.shape
    head_width = width // head_count
    block = head_width * (BLOCK_HEADS if head_count % BLOCK_HEADS == 0 else 1)
    pairs = width // block
    steps = parts * pairs
    row_total, depth = fresh.shape
    whole = pl.BlockSpec(memory_space=pltpu.VMEM)
    kind = fresh.dtype if exchange else jnp.float32
    total = pltpu.VMEM((row_total, own * helper_total), jnp.float32)
    attended = pltpu.VMEM((pairs, row_total, block), jnp.bfloat16)
    extra = [
        pltpu.VMEM((pairs, helper_total, own, block), jnp.bfloat16),
        attended,
        total,
        *[pltpu.SemaphoreType.DMA((pairs,))] * 6,
    ]
    return pl.pallas_call(
        functools.partial(fresh_kernel, head_width),
        out_shape=jax.ShapeDtypeStruct((row_total, own * helper_total), kind),
        in_specs=[whole] * 5,
        out_specs=whole,
        scratch_shapes=[
            pltpu.VMEM((steps, helper_total, own, block), jnp.bfloat16),
            pltpu.VMEM((parts - 1, row_total, block), jnp.float32),
            pltpu.VMEM((head_count, length, length), jnp.float32),
            attended,
            total,
            *(extra if exchange else []),
            *Gather.scratch(steps),
        ],
        compiler_params=pltpu.CompilerParams(
            collective_id=2, has_side_effects=True, vmem_limit_bytes=VMEM_LIMIT
        ),
    )(pieces, fresh, running, running.T, norm_gain.reshape(-1, 1, block))
def local(
    recorded_input_rows,
    out_cotangent,
    fresh_rows,
    seq_counts,
    decay_logs,
    norm_gain,
    qkv_weight,
    emitted_projection_matrix,
    qkv_first,
    qkv_second,
    out_first,
    out_second,
):
    helper_total = lax.axis_size("helper")
    helper = lax.axis_index("helper")
    head_count = decay_logs.shape[0]

    def parts_first(array):
        return jnp.transpose(array, (1, 0, 2))

    weight = parts_first(qkv_weight)
    running = jnp.cumsum(decay_logs, axis=1)
    own_count = jnp.sum(jnp.where(jnp.arange(helper_total) == helper, seq_counts, 0))
    capacity = recorded_input_rows.shape[0] // SEQ_LEN
    live = (jnp.arange(capacity) < own_count).astype(jnp.float32)
    live = jnp.broadcast_to(live[:, None, None], (capacity, 1, qkv_weight.shape[2] // head_count))

    results, turned = replay(
        weight,
        emitted_projection_matrix,
        recorded_input_rows,
        out_cotangent,
        running,
        norm_gain,
        live,
    )
    states = (
        weight,
        emitted_projection_matrix,
        parts_first(qkv_first),
        out_first,
        parts_first(qkv_second),
        out_second,
    )
    pieces, qkv_moment, out_moment = reduce_gradients(turned, results, states, head_count)
    fresh_out = fresh_forward(pieces, fresh_rows, running, norm_gain)
    if fresh_out.dtype != fresh_rows.dtype:
        fresh_out = finish(fresh_out, fresh_rows)
    return (fresh_out, parts_first(qkv_moment), out_moment)


def finish(partial_out, fresh):
    if lax.axis_size("tensor") == 2:
        width = partial_out.shape[1] // 2
        first = lax.axis_index("tensor") == 0
        left, right = partial_out[:, :width], partial_out[:, width:]
        came = swap(jnp.where(first, right, left).astype(jnp.bfloat16), "tensor", 1)
        residual = jnp.where(first, fresh[:, :width], fresh[:, width:])
        piece = residual.astype(jnp.float32) + (jnp.where(first, left, right) + came)
        piece = piece.astype(jnp.bfloat16)
        other = swap(piece, "tensor", 1)
        return jnp.concatenate(
            [jnp.where(first, piece, other), jnp.where(first, other, piece)], axis=1
        )
    share_sum = lax.psum_scatter(partial_out, "tensor", scatter_dimension=1, tiled=True)
    width = share_sum.shape[1]
    residual = lax.dynamic_slice_in_dim(fresh, lax.axis_index("tensor") * width, width, 1)
    piece = (residual.astype(jnp.float32) + share_sum).astype(jnp.bfloat16)
    return lax.all_gather(piece, "tensor", axis=1, tiled=True)


def solution(mesh):
    return jax.shard_map(
        local,
        mesh=mesh,
        in_specs=(
            P("helper", None),
            P("helper", None),
            P("helper", None),
            P(),
            P("tensor", None),
            P("tensor"),
            P("helper", None, "tensor"),
            P("helper", "tensor"),
            P("helper", None, "tensor"),
            P("helper", None, "tensor"),
            P("helper", "tensor"),
            P("helper", "tensor"),
        ),
        out_specs=(P("helper", None), P("helper", None, "tensor"), P("helper", "tensor")),
        check_vma=False,
    )
```

```python
import functools

import jax
import jax.numpy as jnp
from jax import lax
from jax.experimental import pallas as pl
from jax.experimental.pallas import tpu as pltpu
from jax.sharding import PartitionSpec as P


SEQ_LEN = 256


NORM_FLOOR = 1.0
BETA_ONE = 0.9
BETA_TWO = 0.95
ADAM_EPS = 1e-08
LEARN_RATE = 0.005
WEIGHT_DECAY = 0.1
BIAS_ONE = 0.9999734386011124
BIAS_TWO = 0.994079470779666


def multiply(left, right, left_dim, right_dim):
    return lax.dot_general(
        left, right, (((left_dim,), (right_dim,)), ((), ())), preferred_element_type=jnp.float32
    )


def head_forward(raw_query, raw_key, raw_value, mask, gain):
    sigma_query = jax.nn.sigmoid(raw_query)
    sigma_key = jax.nn.sigmoid(raw_key)
    queries = (raw_query * sigma_query).astype(jnp.bfloat16)
    key_rows = (raw_key * sigma_key).astype(jnp.bfloat16)
    values = raw_value.astype(jnp.bfloat16)
    weights = (multiply(queries, key_rows, 1, 1) * mask).astype(jnp.bfloat16)
    mixed = multiply(weights, values, 1, 0)
    mean_square = jnp.mean(mixed * mixed, axis=-1, keepdims=True)
    inverse = lax.rsqrt(jnp.maximum(mean_square, NORM_FLOOR))
    attended = (mixed * inverse * gain).astype(jnp.bfloat16)
    return (
        attended,
        (sigma_query, sigma_key, queries, key_rows, values, weights, mixed, mean_square, inverse),
    )


def adam_step(weight, first_moment, second_moment, gradient):
    first_new = BETA_ONE * first_moment + (1.0 - BETA_ONE) * gradient
    second_new = BETA_TWO * second_moment + (1.0 - BETA_TWO) * gradient * gradient
    update = first_new / BIAS_ONE / (jnp.sqrt(second_new / BIAS_TWO) + ADAM_EPS)
    weight_new = weight - LEARN_RATE * (update + WEIGHT_DECAY * weight)
    return (weight_new.astype(jnp.bfloat16), first_new)


def swap(value, axis, distance):
    count = lax.axis_size(axis)
    return lax.ppermute(value, axis, [(i, i ^ distance) for i in range(count)])


def grouping(count):
    core = 2
    inner = 2
    return count // (core * inner), inner, core


VMEM_LIMIT = 66_000_000
BLOCK_HEADS = 2


def place():
    helper_total = lax.axis_size("helper")
    outer, inner, core = grouping(helper_total)
    helper = lax.axis_index("helper")
    z = helper // (inner * core)
    x = (helper // core) % inner
    c = helper % core

    def at(zz, xx, cc):
        return (zz * inner + xx) * core + cc

    return helper, (outer, inner, core), (z, x, c), at


def remote(source, target, send, recv, peer, axis="helper"):
    return pltpu.make_async_remote_copy(
        src_ref=source,
        dst_ref=target,
        send_sem=send,
        recv_sem=recv,
        device_id={axis: peer},
        device_id_type=pl.DeviceIdType.MESH,
    )


def greet(peers, across=False):
    barrier = pltpu.get_barrier_semaphore()
    targets = [{"helper": peer} for peer in peers]
    if across:
        targets.append({"tensor": 1 - lax.axis_index("tensor")})
    for target in targets:
        pl.semaphore_signal(
            barrier, inc=1, device_id=target, device_id_type=pl.DeviceIdType.MESH
        )
    pl.semaphore_wait(barrier, len(targets))


def helper_peers():
    _, (outer, inner, _), (z, x, c), at = place()
    z_peer = [None] + [at((z + k) % outer, x, c) for k in range(1, outer)]
    x_peer = [None] + [at(z, (x + j) % inner, c) for j in range(1, inner)]
    return z_peer, x_peer, at(z, x, 1 - c)


def each(count, body):
    lax.fori_loop(0, count, lambda i, carry: (body(i), carry)[1], 0)


class Gather:
    def __init__(self, steps, piece_at, full, sems):
        self.steps, self.piece_at, self.full = steps, piece_at, full
        self.z_send, self.z_recv, self.x_send, self.x_recv, self.c_send, self.c_recv = sems
        self.helper, (self.outer, self.inner, _), self.spot, self.at = place()
        self.z_peer, self.x_peer, self.c_peer = helper_peers()
        self.line = self.outer == 4 and self.inner == 2

    @staticmethod
    def scratch(steps):
        outer, inner, _ = grouping(lax.axis_size("helper"))
        sizes = [outer, outer, inner * outer, inner * outer, inner * outer, inner * outer]
        return [pltpu.SemaphoreType.DMA((steps, size)) for size in sizes]

    def peers(self):
        return self.z_peer[1:] + self.x_peer[1:] + [self.c_peer]

    def owner(self, j, k):
        z, x, c = self.spot
        return self.at((z + self.outer - k) % self.outer, (x + self.inner - j) % self.inner, c)

    def source(self, s, j, k):
        return self.full.at[s, self.owner(j, k)] if j or k else self.piece_at(s)

    def z_copy(self, s, k):
        return remote(
            self.piece_at(s),
            self.full.at[s, self.helper],
            self.z_send.at[s, k],
            self.z_recv.at[s, k],
            self.z_peer[k],
        )

    def x_copy(self, s, j, k):
        slot = j * self.outer + k
        return remote(
            self.source(s, 0, k),
            self.full.at[s, self.owner(0, k)],
            self.x_send.at[s, slot],
            self.x_recv.at[s, slot],
            self.x_peer[j],
        )

    def c_copy(self, s, j, k):
        slot = j * self.outer + k
        return remote(
            self.source(s, j, k),
            self.full.at[s, self.owner(j, k)],
            self.c_send.at[s, slot],
            self.c_recv.at[s, slot],
            self.c_peer,
        )

    lag = 2

    def stage(self, s, body):
        pl.when(jnp.logical_and(s >= 0, s < self.steps))(lambda: body(s))


    def z_flow(self, s, k, j):
        if j == 0:
            return self.z_copy(s, k)
        slot = j * self.outer + k
        return remote(
            self.source(s, j, 0),
            self.full.at[s, self.owner(j, 0)],
            self.x_send.at[s, slot],
            self.x_recv.at[s, slot],
            self.z_peer[k],
        )

    def relay(self, s, j, upward):
        send = self.x_send if j else self.z_send
        recv = self.x_recv if j else self.z_recv
        came = self.full.at[s, self.owner(j, 2)]
        return remote(
            came,
            came,
            send.at[s, 0],
            recv.at[s, j * self.outer + (3 if upward else 1)],
            self.z_peer[1 if upward else 3],
        )

    def for_relay(self, s, j, act):
        z = self.spot[0]
        pl.when(z == 1)(lambda: act(self.relay(s, j, False)))
        pl.when(z == 2)(lambda: act(self.relay(s, j, True)))

    def sends(self, k):
        z = self.spot[0]
        return {1: z < self.outer - 1, 2: z >= 0, 3: z > 0}[k]

    def far(self, k):
        z = self.spot[0]
        return {1: z == 0, 3: z == self.outer - 1}[k]

    def z_begin(self, s, j):
        for k in (2, 1, 3):
            pl.when(self.sends(k))(lambda k=k: self.z_flow(s, k, j).start())

    def z_take(self, s, j, then):
        def take(k):
            self.z_flow(s, k, j).wait_recv()
            then(k)

        self.z_flow(s, 2, j).wait_recv()
        self.for_relay(s, j, lambda copy: copy.start())
        then(2)
        for k in (1, 3):
            pl.when(jnp.logical_not(self.far(k)))(functools.partial(take, k))

    def z_late(self, s, j, then):
        def take(k):
            self.z_flow(s, k, j).wait_recv()
            then(k)

        for k in (1, 3):
            pl.when(self.far(k))(functools.partial(take, k))

    def by_order(self, s, z_first, x_first):
        swapped = s % 5 == 1
        pl.when(swapped)(x_first)
        pl.when(jnp.logical_not(swapped))(z_first)

    def begin(self, s):
        if self.line:
            self.z_begin(s, 0)
        else:
            for k in range(1, self.outer):
                self.z_copy(s, k).start()
        for j in range(1, self.inner):
            self.x_copy(s, j, 0).start()
        self.c_copy(s, 0, 0).start()
        self.full[s, self.helper] = self.piece_at(s)[...]

    def spread_x(self, s, k):
        for j in range(1, self.inner):
            self.x_copy(s, j, k).start()
        self.c_copy(s, 0, k).start()

    def after_z(self, s):
        if not self.line:
            for k in range(1, self.outer):
                self.z_copy(s, k).wait_recv()
                self.spread_x(s, k)
            return

        def x_first():
            self.x_copy(s, 1, 0).wait_recv()
            self.z_begin(s, 1)
            self.c_copy(s, 1, 0).start()
            self.z_take(s, 0, lambda k: self.c_copy(s, 0, k).start())

        self.by_order(s, lambda: self.z_take(s, 0, functools.partial(self.spread_x, s)), x_first)

    def after_x(self, s):
        def take(k):
            for j in range(1, self.inner):
                self.x_copy(s, j, k).wait_recv()
                self.c_copy(s, j, k).start()

        if not self.line:
            for k in range(self.outer):
                take(k)
            return

        def z_first():
            self.z_late(s, 0, functools.partial(self.spread_x, s))
            take(0)
            take(2)
            for k in (1, 3):
                pl.when(jnp.logical_not(self.far(k)))(functools.partial(take, k))
            for k in (1, 3):
                pl.when(self.far(k))(functools.partial(take, k))

        def x_first():
            self.z_late(s, 0, lambda k: self.c_copy(s, 0, k).start())
            self.z_take(s, 1, lambda k: self.c_copy(s, 1, k).start())
            self.z_late(s, 1, lambda k: self.c_copy(s, 1, k).start())

        self.by_order(s, z_first, x_first)

    def after_c(self, s):
        for k in range(self.outer):
            for j in range(self.inner):
                self.c_copy(s, j, k).wait_recv()

    def tick(self, t):
        self.stage(t + 1, self.begin)
        self.stage(t - 1, self.after_z)
        self.stage(t - 2, self.after_x)

    def finish(self):
        def z_sent(s, j):
            for k in (1, 2, 3):
                pl.when(self.sends(k))(lambda k=k: self.z_flow(s, k, j).wait_send())
            self.for_relay(s, j, lambda copy: copy.wait_send())

        def x_sent(s):
            for k in range(1, self.outer):
                for j in range(1, self.inner):
                    self.x_copy(s, j, k).wait_send()

        def drain(s):
            for j in range(1, self.inner):
                self.x_copy(s, j, 0).wait_send()
            for k in range(self.outer):
                for j in range(self.inner):
                    self.c_copy(s, j, k).wait_send()
            if self.line:
                z_sent(s, 0)
                self.by_order(s, lambda: x_sent(s), lambda: z_sent(s, 1))
            else:
                x_sent(s)
                for k in range(1, self.outer):
                    self.z_copy(s, k).wait_send()

        each(self.steps, drain)


def columns(p, width):
    return pl.ds(pl.multiple_of(p * width, width), width)


def fill_mask(mask, across, down):
    length = mask.shape[1]
    later = lax.broadcasted_iota(jnp.int32, (length, length), 0) >= lax.broadcasted_iota(
        jnp.int32, (length, length), 1
    )
    for n in range(mask.shape[0]):
        spread_factor = down[:, n : n + 1] - across[n : n + 1, :]
        mask[n] = jnp.where(later, jnp.exp(jnp.where(later, spread_factor, 0.0)), 0.0)


def head_backward(kept, raw_query, raw_key, cotangent, decay, gain_row):
    sigma_query, sigma_key, queries, key_rows, values, weights, mixed, square, inverse = kept
    active = jnp.where(square > NORM_FLOOR, 1.0, 0.0)
    scaled = cotangent * gain_row
    grad_mixed = inverse * scaled - active * mixed * (inverse * inverse * inverse) * jnp.mean(
        scaled * mixed, axis=-1, keepdims=True
    )
    grad_mixed = grad_mixed.astype(jnp.bfloat16)
    grad_scores = (multiply(grad_mixed, values, 1, 1) * decay).astype(jnp.bfloat16)
    grad_value = multiply(weights, grad_mixed, 0, 0)
    grad_query = multiply(grad_scores, key_rows, 1, 0)
    grad_key = multiply(grad_scores, queries, 0, 0)
    grad_query = grad_query * sigma_query * (1.0 + raw_query * (1.0 - sigma_query))
    grad_key = grad_key * sigma_key * (1.0 + raw_key * (1.0 - sigma_key))
    return grad_query, grad_key, grad_value


def replay_kernel(
    head_width,
    qkv_weight,
    out_weight,
    logged,
    cotangent,
    across,
    down,
    gain,
    live,
    results,
    turned,
    piece,
    mask,
    rows,
    full,
    raw,
    found,
    flipped,
    row_sem,
    found_sem,
    flip_sem,
    *sems,
):
    parts, _, width = piece.shape
    block = full.shape[-1]
    pairs = width // block
    steps = parts * pairs
    capacity = live.shape[0]
    length = mask.shape[1]
    depth = rows.shape[2]
    gather = Gather(steps, lambda s: piece.at[s % parts, :, columns(s // parts, block)], full, sems)
    loads = [
        pltpu.make_async_copy(source, rows.at[i], row_sem.at[i])
        for i, source in enumerate((logged, cotangent))
    ]
    for load in loads:
        load.start()
    for m in range(parts - 1):
        piece[m] = qkv_weight[m].astype(jnp.bfloat16)
    piece[parts - 1] = out_weight[...].astype(jnp.bfloat16)
    greet(gather.peers())
    gather.begin(0)
    gather.stage(1, gather.begin)
    fill_mask(mask, across, down)
    for load in loads:
        load.wait()

    flips = depth // block
    flip_ticks = 4
    flip_share = -(-2 * flips // flip_ticks)

    def flip_copy(i):
        slot = i % 2
        return pltpu.make_async_copy(
            flipped.at[slot],
            turned.at[i // flips, columns(i % flips, block)],
            flip_sem.at[slot],
        )

    def flip(i):
        pl.when(i >= 2)(lambda: flip_copy(i - 2).wait())
        at = columns(i % flips, block)
        for j in range(capacity):
            part = pl.ds(j * length, length)
            flipped[i % 2, :, part] = rows[i // flips, part, at].T
        flip_copy(i).start()

    def found_copy(p, m):
        slot = p % 2
        return pltpu.make_async_copy(
            found.at[slot, m], results.at[m, :, columns(p, block)], found_sem.at[slot, m]
        )

    share = -(-capacity // parts)

    def heads(p, m):
        slot = p % 2

        @pl.when(jnp.logical_and(m == 0, p >= 2))
        def _():
            for i in range(parts):
                found_copy(p - 2, i).wait()

        def one(j):
            part = pl.ds(pl.multiple_of(j * length, length), length)
            alive = live[j] > 0.5
            for n in range(block // head_width):
                at = slice(n * head_width, (n + 1) * head_width)
                decay = mask[p * (block // head_width) + n]
                gain_row = gain[p, :, at]
                raw_query, raw_key = raw[slot, 0, part, at], raw[slot, 1, part, at]
                attended, kept = head_forward(
                    raw_query, raw_key, raw[slot, 2, part, at], decay, gain_row
                )
                grads = head_backward(
                    kept, raw_query, raw_key, raw[slot, 3, part, at], decay, gain_row
                )
                for i, result in enumerate((*grads, attended.astype(jnp.float32))):
                    found[slot, i, part, at] = jnp.where(alive, result, 0.0).astype(jnp.bfloat16)

        for i in range(share):
            j = m * share + i
            pl.when(j < capacity)(functools.partial(one, j))

        @pl.when(m == parts - 1)
        def _():
            for i in range(parts):
                found_copy(p, i).start()

    def product(s):
        m = s % parts
        p = s // parts
        source = jnp.where(m == parts - 1, 1, 0)

        def one(j):
            part = pl.ds(pl.multiple_of(j * length, length), length)
            weight = full[s].reshape(depth, block)
            raw[p % 2, m, part] = multiply(rows[source, part, :], weight, 1, 0)

        each(capacity, one)

    def step(t):
        pl.when(t > 0)(lambda: gather.tick(t))

        @pl.when(t < flip_ticks)
        def _():
            for i in range(flip_share):
                pl.when(t * flip_share + i < 2 * flips)(lambda i=i: flip(t * flip_share + i))

        s = t - gather.lag
        pl.when(s >= parts)(lambda: heads(s // parts - 1, s % parts))

        @pl.when(jnp.logical_and(s >= 0, s < steps))
        def _():
            gather.after_c(s)
            product(s)

    each(steps + parts + gather.lag, step)
    for i in range(2 * flips - 2, 2 * flips):
        flip_copy(i).wait()
    for p in range(max(pairs - 2, 0), pairs):
        for m in range(parts):
            found_copy(p, m).wait()
    gather.finish()


def replay(qkv_weight, out_weight, logged, cotangent, running, norm_gain, live):
    helper_total = lax.axis_size("helper")
    parts, own, width = qkv_weight.shape[0] + 1, *out_weight.shape
    head_count, length = running.shape
    head_width = width // head_count
    block = head_width * (BLOCK_HEADS if head_count % BLOCK_HEADS == 0 else 1)
    steps = parts * (width // block)
    row_total, depth = logged.shape
    dma = pltpu.SemaphoreType.DMA
    whole = pl.BlockSpec(memory_space=pltpu.VMEM)
    away = pl.BlockSpec(memory_space=pl.ANY)
    return pl.pallas_call(
        functools.partial(replay_kernel, head_width),
        out_shape=[
            jax.ShapeDtypeStruct((parts, row_total, width), jnp.bfloat16),
            jax.ShapeDtypeStruct((2, depth, row_total), jnp.bfloat16),
        ],
        in_specs=[whole, whole, away, away, whole, whole, whole, whole],
        out_specs=[away, away],
        scratch_shapes=[
            pltpu.VMEM((parts, own, width), jnp.bfloat16),
            pltpu.VMEM((head_count, length, length), jnp.float32),
            pltpu.VMEM((2, row_total, depth), jnp.bfloat16),
            pltpu.VMEM((steps, helper_total, own, block), jnp.bfloat16),
            pltpu.VMEM((2, parts, row_total, block), jnp.float32),
            pltpu.VMEM((2, parts, row_total, block), jnp.bfloat16),
            pltpu.VMEM((2, block, row_total), jnp.bfloat16),
            dma((2,)),
            dma((2, parts)),
            dma((2,)),
            *Gather.scratch(steps),
        ],
        compiler_params=pltpu.CompilerParams(
            collective_id=0, has_side_effects=True, vmem_limit_bytes=VMEM_LIMIT
        ),
    )(
        qkv_weight,
        out_weight,
        logged,
        cotangent,
        running,
        running.T,
        norm_gain.reshape(-1, 1, block),
        live,
    )


def reduce_kernel(
    turned,
    results,
    qkv_weight_far,
    out_weight_far,
    qkv_first_far,
    out_first_far,
    qkv_second_far,
    out_second_far,
    pieces,
    qkv_moment,
    out_moment,
    left,
    right,
    own,
    core_out,
    core_in,
    own_x,
    x_out,
    x_in,
    own_z,
    z_out,
    z_in,
    left_sem,
    right_sem,
    c_send,
    c_recv,
    x_send,
    x_recv,
    z_send,
    z_recv,
    qkv_weight,
    out_weight,
    qkv_first,
    out_first,
    qkv_second,
    out_second,
    state_sem,
):
    states = [
        pltpu.make_async_copy(source, target, state_sem.at[i])
        for i, (source, target) in enumerate(
            (
                (qkv_weight_far, qkv_weight),
                (out_weight_far, out_weight),
                (qkv_first_far, qkv_first),
                (out_first_far, out_first),
                (qkv_second_far, qkv_second),
                (out_second_far, out_second),
            )
        )
    ]
    parts, _, width = results.shape
    block = right.shape[-1]
    pairs = width // block
    steps = parts * pairs
    size = out_weight.shape[0]
    _, (outer, inner, core), (z, x, c), _ = place()
    z_peer, x_peer, c_peer = helper_peers()

    def load_right(s):
        return pltpu.make_async_copy(
            results.at[s % parts, :, columns(s // parts, block)], right.at[s], right_sem.at[s]
        )

    def load_left(i):
        return pltpu.make_async_copy(turned.at[i], left.at[i], left_sem.at[i])

    load_left(0).start()
    load_right(0).start()
    for s in range(1, parts):
        load_right(s).start()
    load_left(1).start()
    for s in range(parts, steps):
        load_right(s).start()
    for state in states:
        state.start()
    greet(z_peer[1:] + x_peer[1:] + [c_peer])

    def c_copy(s):
        return remote(core_out.at[s % 2], core_in.at[s], c_send.at[s], c_recv.at[s], c_peer)

    def x_copy(s, j):
        return remote(
            x_out.at[s % 2, j], x_in.at[s, j], x_send.at[s, j], x_recv.at[s, j], x_peer[j]
        )

    def z_copy(s, k):
        return remote(
            z_out.at[s % 2, k], z_in.at[s, k], z_send.at[s, k], z_recv.at[s, k], z_peer[k]
        )

    def begin(s):
        load_right(s).wait()
        pl.when(s == 0)(lambda: load_left(0).wait())
        pl.when(s == parts - 1)(lambda: load_left(1).wait())
        pl.when(s >= 2)(lambda: c_copy(s - 2).wait_send())
        source = jnp.where(s % parts == parts - 1, 1, 0)
        slot = s % 2

        def one(q):
            span = core * size
            part = pl.ds(pl.multiple_of(q * span, span), span)
            total = multiply(left[source, part, :], right[s], 1, 0)
            first, second = total[:size], total[size:]
            own[slot, q] = jnp.where(c == 0, first, second)
            core_out[slot, q] = jnp.where(c == 0, second, first).astype(jnp.bfloat16)

        each(outer * inner, one)
        c_copy(s).start()

    def after_c(s):
        c_copy(s).wait_recv()
        slot = s % 2

        @pl.when(s >= 2)
        def _():
            for j in range(1, inner):
                x_copy(s - 2, j).wait_send()

        for j in range(1, inner):
            for k in range(outer):
                q = k * inner + (x + j) % inner
                x_out[slot, j, k] = (own[slot, q] + core_in[s, q]).astype(jnp.bfloat16)
            x_copy(s, j).start()
        for k in range(outer):
            q = k * inner + x
            own_x[slot, k] = own[slot, q] + core_in[s, q]

    def after_x(s):
        slot = s % 2
        for j in range(1, inner):
            x_copy(s, j).wait_recv()

        @pl.when(s >= 2)
        def _():
            for k in range(1, outer):
                z_copy(s - 2, k).wait_send()

        def total(q):
            value = own_x[slot, q]
            for j in range(1, inner):
                value = value + x_in[s, j, q]
            return value

        for k in range(1, outer):
            z_out[slot, k] = total((z + k) % outer).astype(jnp.bfloat16)
            z_copy(s, k).start()
        own_z[slot] = total(z)

    def after_z(s):
        @pl.when(s == 0)
        def _():
            for state in states:
                state.wait()

        value = own_z[s % 2]
        for k in range(1, outer):
            z_copy(s, k).wait_recv()
            value = value + z_in[s, k]
        m = s % parts
        at = columns(s // parts, block)

        @pl.when(m < parts - 1)
        def _():
            piece, moment = adam_step(
                qkv_weight[m, :, at], qkv_first[m, :, at], qkv_second[m, :, at], value
            )
            pieces[m, :, at] = piece
            qkv_moment[m, :, at] = moment

        @pl.when(m == parts - 1)
        def _():
            piece, moment = adam_step(
                out_weight[:, at], out_first[:, at], out_second[:, at], value
            )
            pieces[m, :, at] = piece
            out_moment[:, at] = moment

    def step(t):
        for lag, body in enumerate((begin, after_c, after_x, after_z)):
            s = t - lag
            pl.when(jnp.logical_and(s >= 0, s < steps))(functools.partial(body, s))

    each(steps + 3, step)
    for s in range(max(steps - 2, 0), steps):
        c_copy(s).wait_send()
        for j in range(1, inner):
            x_copy(s, j).wait_send()
        for k in range(1, outer):
            z_copy(s, k).wait_send()


def reduce_gradients(turned, results, states, head_count):
    helper_total = lax.axis_size("helper")
    outer, inner, core = grouping(helper_total)
    parts, row_total, width = results.shape
    depth = turned.shape[1]
    size = depth // helper_total
    block = width // head_count * (BLOCK_HEADS if head_count % BLOCK_HEADS == 0 else 1)
    steps = parts * (width // block)
    dma = pltpu.SemaphoreType.DMA
    half, full = jnp.bfloat16, jnp.float32
    tile = (size, block)
    whole = pl.BlockSpec(memory_space=pltpu.VMEM)
    away = pl.BlockSpec(memory_space=pl.ANY)
    return pl.pallas_call(
        reduce_kernel,
        out_shape=[
            jax.ShapeDtypeStruct((parts, size, width), half),
            jax.ShapeDtypeStruct((parts - 1, size, width), full),
            jax.ShapeDtypeStruct((size, width), full),
        ],
        in_specs=[away] * 8,
        out_specs=[whole] * 3,
        scratch_shapes=[
            pltpu.VMEM((2, depth, row_total), half),
            pltpu.VMEM((steps, row_total, block), half),
            pltpu.VMEM((2, outer * inner, *tile), full),
            pltpu.VMEM((2, outer * inner, *tile), half),
            pltpu.VMEM((steps, outer * inner, *tile), half),
            pltpu.VMEM((2, outer, *tile), full),
            pltpu.VMEM((2, inner, outer, *tile), half),
            pltpu.VMEM((steps, inner, outer, *tile), half),
            pltpu.VMEM((2, *tile), full),
            pltpu.VMEM((2, outer, *tile), half),
            pltpu.VMEM((steps, outer, *tile), half),
            dma((2,)),
            dma((steps,)),
            dma((steps,)),
            dma((steps,)),
            dma((steps, inner)),
            dma((steps, inner)),
            dma((steps, outer)),
            dma((steps, outer)),
            *[pltpu.VMEM(state.shape, state.dtype) for state in states],
            dma((len(states),)),
        ],
        compiler_params=pltpu.CompilerParams(
            collective_id=1, has_side_effects=True, vmem_limit_bytes=VMEM_LIMIT
        ),
    )(turned, results, *states)


def fresh_kernel(head_width, piece, fresh, across, down, gain, out, *scratch):
    exchange = out.dtype == fresh.dtype
    full, raw, mask, attended, total = scratch[:5]
    sems = scratch[5:]
    if exchange:
        other, other_attended, other_total, *marks = scratch[5:14]
        sems = scratch[14:]
    parts, _, width = piece.shape
    block = full.shape[-1]
    pairs = width // block
    steps = parts * pairs
    depth = fresh.shape[1]

    def piece_at(s):
        later = s - pairs
        m = jnp.where(later < 0, parts - 1, later % (parts - 1))
        p = jnp.where(later < 0, s, later // (parts - 1))
        return piece.at[m, :, columns(p, block)]

    gather = Gather(steps, piece_at, full, sems)
    greet(gather.peers(), exchange)
    gather.begin(0)
    gather.stage(1, gather.begin)
    fill_mask(mask, across, down)
    total[...] = jnp.zeros_like(total)
    if exchange:
        other_total[...] = jnp.zeros_like(other_total)
        partner = 1 - lax.axis_index("tensor")
        y_send, y_recv, c_send, c_recv, a_send, a_recv = marks
        share = full.shape[1] // 2
        half = pl.ds(pl.multiple_of(gather.spot[2] * share, share), share)

        def y_copy(p):
            return remote(
                full.at[p, half], other.at[p, half], y_send.at[p], y_recv.at[p], partner, "tensor"
            )

        def c_copy(p):
            return remote(
                other.at[p, half], other.at[p, half], c_send.at[p], c_recv.at[p], gather.c_peer
            )

        def a_copy(p):
            return remote(
                attended.at[p], other_attended.at[p], a_send.at[p], a_recv.at[p], partner, "tensor"
            )

        def take_other(p):
            a_copy(p).wait_recv()
            c_copy(p).wait_recv()
            weight = other[p].reshape(depth, block)
            other_total[...] += multiply(other_attended[p], weight, 1, 1)

        def relay(i):
            y_copy(i).wait_recv()
            c_copy(i).start()

    def heads(p):
        for n in range(block // head_width):
            at = slice(n * head_width, (n + 1) * head_width)
            decay = mask[p * (block // head_width) + n]
            attended[p, :, at] = head_forward(
                raw[0, :, at], raw[1, :, at], raw[2, :, at], decay, gain[p, :, at]
            )[0]
        if exchange:
            a_copy(p).start()
        total[...] += multiply(attended[p], full[p].reshape(depth, block), 1, 1)
        if exchange:
            pl.when(p > 0)(lambda: take_other(p - 1))

    def compute(s):
        gather.after_c(s)
        if exchange:
            pl.when(s < pairs)(lambda: y_copy(s).start())
            since = s - 3
            turn = jnp.logical_and(since >= 0, since < 2 * pairs)
            pl.when(jnp.logical_and(turn, since % 2 == 0))(lambda: relay(since // 2))

        @pl.when(s >= pairs)
        def _():
            m = (s - pairs) % (parts - 1)
            raw[m] = multiply(fresh[...], full[s].reshape(depth, block), 1, 0)
            pl.when(m == parts - 2)(lambda: heads((s - pairs) // (parts - 1)))

    def step(t):
        pl.when(t > 0)(lambda: gather.tick(t))
        pl.when(t >= gather.lag)(lambda: compute(t - gather.lag))

    each(steps + gather.lag, step)
    if exchange:
        for p in range(pairs):
            if 3 + 2 * p >= steps:
                relay(p)
        take_other(pairs - 1)
        summed = total[...] + other_total[...]
        out[...] = (fresh[...].astype(jnp.float32) + summed).astype(out.dtype)
        for p in range(pairs):
            y_copy(p).wait_send()
            c_copy(p).wait_send()
            a_copy(p).wait_send()
    else:
        out[...] = total[...]
    gather.finish()


def fresh_forward(pieces, fresh, running, norm_gain):
    helper_total = lax.axis_size("helper")
    exchange = lax.axis_size("tensor") == 2
    parts, own, width = pieces.shape
    head_count, length = running.shape
    head_width = width // head_count
    block = head_width * (BLOCK_HEADS if head_count % BLOCK_HEADS == 0 else 1)
    pairs = width // block
    steps = parts * pairs
    row_total, depth = fresh.shape
    whole = pl.BlockSpec(memory_space=pltpu.VMEM)
    kind = fresh.dtype if exchange else jnp.float32
    total = pltpu.VMEM((row_total, own * helper_total), jnp.float32)
    attended = pltpu.VMEM((pairs, row_total, block), jnp.bfloat16)
    extra = [
        pltpu.VMEM((pairs, helper_total, own, block), jnp.bfloat16),
        attended,
        total,
        *[pltpu.SemaphoreType.DMA((pairs,))] * 6,
    ]
    return pl.pallas_call(
        functools.partial(fresh_kernel, head_width),
        out_shape=jax.ShapeDtypeStruct((row_total, own * helper_total), kind),
        in_specs=[whole] * 5,
        out_specs=whole,
        scratch_shapes=[
            pltpu.VMEM((steps, helper_total, own, block), jnp.bfloat16),
            pltpu.VMEM((parts - 1, row_total, block), jnp.float32),
            pltpu.VMEM((head_count, length, length), jnp.float32),
            attended,
            total,
            *(extra if exchange else []),
            *Gather.scratch(steps),
        ],
        compiler_params=pltpu.CompilerParams(
            collective_id=2, has_side_effects=True, vmem_limit_bytes=VMEM_LIMIT
        ),
    )(pieces, fresh, running, running.T, norm_gain.reshape(-1, 1, block))
def local(
    recorded_input_rows,
    out_cotangent,
    fresh_rows,
    seq_counts,
    decay_logs,
    norm_gain,
    qkv_weight,
    emitted_projection_matrix,
    qkv_first,
    qkv_second,
    out_first,
    out_second,
):
    helper_total = lax.axis_size("helper")
    helper = lax.axis_index("helper")
    head_count = decay_logs.shape[0]

    def parts_first(array):
        return jnp.transpose(array, (1, 0, 2))

    weight = parts_first(qkv_weight)
    running = jnp.cumsum(decay_logs, axis=1)
    own_count = jnp.sum(jnp.where(jnp.arange(helper_total) == helper, seq_counts, 0))
    capacity = recorded_input_rows.shape[0] // SEQ_LEN
    live = (jnp.arange(capacity) < own_count).astype(jnp.float32)
    live = jnp.broadcast_to(live[:, None, None], (capacity, 1, qkv_weight.shape[2] // head_count))

    results, turned = replay(
        weight,
        emitted_projection_matrix,
        recorded_input_rows,
        out_cotangent,
        running,
        norm_gain,
        live,
    )
    states = (
        weight,
        emitted_projection_matrix,
        parts_first(qkv_first),
        out_first,
        parts_first(qkv_second),
        out_second,
    )
    pieces, qkv_moment, out_moment = reduce_gradients(turned, results, states, head_count)
    fresh_out = fresh_forward(pieces, fresh_rows, running, norm_gain)
    if fresh_out.dtype != fresh_rows.dtype:
        fresh_out = finish(fresh_out, fresh_rows)
    return (fresh_out, parts_first(qkv_moment), out_moment)


def finish(partial_out, fresh):
    if lax.axis_size("tensor") == 2:
        width = partial_out.shape[1] // 2
        first = lax.axis_index("tensor") == 0
        left, right = partial_out[:, :width], partial_out[:, width:]
        came = swap(jnp.where(first, right, left).astype(jnp.bfloat16), "tensor", 1)
        residual = jnp.where(first, fresh[:, :width], fresh[:, width:])
        piece = residual.astype(jnp.float32) + (jnp.where(first, left, right) + came)
        piece = piece.astype(jnp.bfloat16)
        other = swap(piece, "tensor", 1)
        return jnp.concatenate(
            [jnp.where(first, piece, other), jnp.where(first, other, piece)], axis=1
        )
    share_sum = lax.psum_scatter(partial_out, "tensor", scatter_dimension=1, tiled=True)
    width = share_sum.shape[1]
    residual = lax.dynamic_slice_in_dim(fresh, lax.axis_index("tensor") * width, width, 1)
    piece = (residual.astype(jnp.float32) + share_sum).astype(jnp.bfloat16)
    return lax.all_gather(piece, "tensor", axis=1, tiled=True)


def solution(mesh):
    return jax.shard_map(
        local,
        mesh=mesh,
        in_specs=(
            P("helper", None),
            P("helper", None),
            P("helper", None),
            P(),
            P("tensor", None),
            P("tensor"),
            P("helper", None, "tensor"),
            P("helper", "tensor"),
            P("helper", None, "tensor"),
            P("helper", None, "tensor"),
            P("helper", "tensor"),
            P("helper", "tensor"),
        ),
        out_specs=(P("helper", None), P("helper", None, "tensor"), P("helper", "tensor")),
        check_vma=False,
    )
```

```python
import functools

import jax
import jax.numpy as jnp
from jax import lax
from jax.experimental import pallas as pl
from jax.experimental.pallas import tpu as pltpu
from jax.sharding import PartitionSpec as P


SEQ_LEN = 256


NORM_FLOOR = 1.0
BETA_ONE = 0.9
BETA_TWO = 0.95
ADAM_EPS = 1e-08
LEARN_RATE = 0.005
WEIGHT_DECAY = 0.1
BIAS_ONE = 0.9999734386011124
BIAS_TWO = 0.994079470779666


def multiply(left, right, left_dim, right_dim):
    return lax.dot_general(
        left, right, (((left_dim,), (right_dim,)), ((), ())), preferred_element_type=jnp.float32
    )


def head_forward(raw_query, raw_key, raw_value, mask, gain):
    sigma_query = jax.nn.sigmoid(raw_query)
    sigma_key = jax.nn.sigmoid(raw_key)
    queries = (raw_query * sigma_query).astype(jnp.bfloat16)
    key_rows = (raw_key * sigma_key).astype(jnp.bfloat16)
    values = raw_value.astype(jnp.bfloat16)
    weights = (multiply(queries, key_rows, 1, 1) * mask).astype(jnp.bfloat16)
    mixed = multiply(weights, values, 1, 0)
    mean_square = jnp.mean(mixed * mixed, axis=-1, keepdims=True)
    inverse = lax.rsqrt(jnp.maximum(mean_square, NORM_FLOOR))
    attended = (mixed * inverse * gain).astype(jnp.bfloat16)
    return (
        attended,
        (sigma_query, sigma_key, queries, key_rows, values, weights, mixed, mean_square, inverse),
    )


def adam_step(weight, first_moment, second_moment, gradient):
    first_new = BETA_ONE * first_moment + (1.0 - BETA_ONE) * gradient
    second_new = BETA_TWO * second_moment + (1.0 - BETA_TWO) * gradient * gradient
    update = first_new / BIAS_ONE / (jnp.sqrt(second_new / BIAS_TWO) + ADAM_EPS)
    weight_new = weight - LEARN_RATE * (update + WEIGHT_DECAY * weight)
    return (weight_new.astype(jnp.bfloat16), first_new)


def swap(value, axis, distance):
    count = lax.axis_size(axis)
    return lax.ppermute(value, axis, [(i, i ^ distance) for i in range(count)])


def grouping(count):
    core = 2
    inner = 2
    return count // (core * inner), inner, core


VMEM_LIMIT = 66_000_000
BLOCK_HEADS = 2


def place():
    helper_total = lax.axis_size("helper")
    outer, inner, core = grouping(helper_total)
    helper = lax.axis_index("helper")
    z = helper // (inner * core)
    x = (helper // core) % inner
    c = helper % core

    def at(zz, xx, cc):
        return (zz * inner + xx) * core + cc

    return helper, (outer, inner, core), (z, x, c), at


def remote(source, target, send, recv, peer, axis="helper"):
    return pltpu.make_async_remote_copy(
        src_ref=source,
        dst_ref=target,
        send_sem=send,
        recv_sem=recv,
        device_id={axis: peer},
        device_id_type=pl.DeviceIdType.MESH,
    )


def greet(peers, across=False):
    barrier = pltpu.get_barrier_semaphore()
    targets = [{"helper": peer} for peer in peers]
    if across:
        targets.append({"tensor": 1 - lax.axis_index("tensor")})
    for target in targets:
        pl.semaphore_signal(
            barrier, inc=1, device_id=target, device_id_type=pl.DeviceIdType.MESH
        )
    pl.semaphore_wait(barrier, len(targets))


def helper_peers():
    _, (outer, inner, _), (z, x, c), at = place()
    z_peer = [None] + [at((z + k) % outer, x, c) for k in range(1, outer)]
    x_peer = [None] + [at(z, (x + j) % inner, c) for j in range(1, inner)]
    return z_peer, x_peer, at(z, x, 1 - c)


def each(count, body):
    lax.fori_loop(0, count, lambda i, carry: (body(i), carry)[1], 0)


class Gather:
    def __init__(self, steps, piece_at, full, sems):
        self.steps, self.piece_at, self.full = steps, piece_at, full
        self.z_send, self.z_recv, self.x_send, self.x_recv, self.c_send, self.c_recv = sems
        self.helper, (self.outer, self.inner, _), self.spot, self.at = place()
        self.z_peer, self.x_peer, self.c_peer = helper_peers()

    @staticmethod
    def scratch(steps):
        outer, inner, _ = grouping(lax.axis_size("helper"))
        sizes = [outer, outer, inner * outer, inner * outer, inner * outer, inner * outer]
        return [pltpu.SemaphoreType.DMA((steps, size)) for size in sizes]

    def peers(self):
        return self.z_peer[1:] + self.x_peer[1:] + [self.c_peer]

    def owner(self, j, k):
        z, x, c = self.spot
        return self.at((z + self.outer - k) % self.outer, (x + self.inner - j) % self.inner, c)

    def source(self, s, j, k):
        return self.full.at[s, self.owner(j, k)] if j or k else self.piece_at(s)

    def z_copy(self, s, k):
        return remote(
            self.piece_at(s),
            self.full.at[s, self.helper],
            self.z_send.at[s, k],
            self.z_recv.at[s, k],
            self.z_peer[k],
        )

    def x_copy(self, s, j, k):
        slot = j * self.outer + k
        return remote(
            self.source(s, 0, k),
            self.full.at[s, self.owner(0, k)],
            self.x_send.at[s, slot],
            self.x_recv.at[s, slot],
            self.x_peer[j],
        )

    def c_copy(self, s, j, k):
        slot = j * self.outer + k
        return remote(
            self.source(s, j, k),
            self.full.at[s, self.owner(j, k)],
            self.c_send.at[s, slot],
            self.c_recv.at[s, slot],
            self.c_peer,
        )

    lag = 2
    ahead = 3

    def stage(self, s, body):
        pl.when(jnp.logical_and(s >= 0, s < self.steps))(lambda: body(s))

    def begin(self, s):
        for k in range(1, self.outer):
            self.z_copy(s, k).start()
        self.c_copy(s, 0, 0).start()
        self.full[s, self.helper] = self.piece_at(s)[...]

    def begin_x(self, s):
        for j in range(1, self.inner):
            self.x_copy(s, j, 0).start()

    def open(self):
        self.stage(0, self.begin)
        for s in range(self.ahead + 1):
            self.stage(s, self.begin_x)
        self.stage(1, self.begin)

    def after_z(self, s):
        for k in range(1, self.outer):
            self.z_copy(s, k).wait_recv()
            for j in range(1, self.inner):
                self.x_copy(s, j, k).start()
            self.c_copy(s, 0, k).start()

    def after_x(self, s):
        for k in range(self.outer):
            for j in range(1, self.inner):
                self.x_copy(s, j, k).wait_recv()
                self.c_copy(s, j, k).start()

    def after_c(self, s):
        for k in range(self.outer):
            for j in range(self.inner):
                self.c_copy(s, j, k).wait_recv()

    def tick(self, t):
        self.stage(t + 1, self.begin)
        self.stage(t + self.ahead, self.begin_x)
        self.stage(t - 1, self.after_z)
        self.stage(t - 2, self.after_x)

    def finish(self):
        def drain(s):
            for k in range(self.outer):
                if k:
                    self.z_copy(s, k).wait_send()
                for j in range(self.inner):
                    if j:
                        self.x_copy(s, j, k).wait_send()
                    self.c_copy(s, j, k).wait_send()

        each(self.steps, drain)


def columns(p, width):
    return pl.ds(pl.multiple_of(p * width, width), width)


def fill_mask(mask, decay_logs):
    length = mask.shape[1]
    down = lax.broadcasted_iota(jnp.int32, (length, length), 0)
    across = lax.broadcasted_iota(jnp.int32, (length, length), 1)
    later = down >= across
    for n in range(mask.shape[0]):
        logs = jnp.broadcast_to(decay_logs[n : n + 1, :], (length, length))
        running = jnp.sum(jnp.where(later, logs, 0.0), axis=1, keepdims=True)
        running = jnp.broadcast_to(running, (length, length))
        turned = jnp.sum(jnp.where(down == across, running, 0.0), axis=0, keepdims=True)
        spread_factor = running - turned
        mask[n] = jnp.where(later, jnp.exp(jnp.where(later, spread_factor, 0.0)), 0.0)


def head_backward(kept, raw_query, raw_key, cotangent, decay, gain_row):
    sigma_query, sigma_key, queries, key_rows, values, weights, mixed, square, inverse = kept
    active = jnp.where(square > NORM_FLOOR, 1.0, 0.0)
    scaled = cotangent * gain_row
    grad_mixed = inverse * scaled - active * mixed * (inverse * inverse * inverse) * jnp.mean(
        scaled * mixed, axis=-1, keepdims=True
    )
    grad_mixed = grad_mixed.astype(jnp.bfloat16)
    grad_scores = (multiply(grad_mixed, values, 1, 1) * decay).astype(jnp.bfloat16)
    grad_value = multiply(weights, grad_mixed, 0, 0)
    grad_query = multiply(grad_scores, key_rows, 1, 0)
    grad_key = multiply(grad_scores, queries, 0, 0)
    grad_query = grad_query * sigma_query * (1.0 + raw_query * (1.0 - sigma_query))
    grad_key = grad_key * sigma_key * (1.0 + raw_key * (1.0 - sigma_key))
    return grad_query, grad_key, grad_value


def replay_kernel(
    head_width,
    qkv_weight,
    out_weight,
    logged,
    cotangent,
    decay_logs,
    gain,
    counts,
    results,
    turned,
    piece,
    mask,
    rows,
    full,
    raw,
    found,
    flipped,
    row_sem,
    found_sem,
    flip_sem,
    *sems,
):
    parts, _, width = piece.shape
    block = full.shape[-1]
    pairs = width // block
    steps = parts * pairs
    length = mask.shape[1]
    depth = rows.shape[2]
    capacity = rows.shape[1] // length
    count = jnp.full((1, head_width), counts[lax.axis_index("helper")], jnp.int32)
    gather = Gather(steps, lambda s: piece.at[s % parts, :, columns(s // parts, block)], full, sems)
    loads = [
        pltpu.make_async_copy(source, rows.at[i], row_sem.at[i])
        for i, source in enumerate((logged, cotangent))
    ]
    for load in loads:
        load.start()
    for m in range(parts - 1):
        piece[m] = qkv_weight[m].astype(jnp.bfloat16)
    piece[parts - 1] = out_weight[...].astype(jnp.bfloat16)
    greet(gather.peers())
    gather.open()
    fill_mask(mask, decay_logs)
    for load in loads:
        load.wait()

    flips = depth // block
    flip_ticks = 4
    flip_share = -(-2 * flips // flip_ticks)

    def flip_copy(i):
        slot = i % 2
        return pltpu.make_async_copy(
            flipped.at[slot],
            turned.at[i // flips, columns(i % flips, block)],
            flip_sem.at[slot],
        )

    def flip(i):
        pl.when(i >= 2)(lambda: flip_copy(i - 2).wait())
        at = columns(i % flips, block)
        for j in range(capacity):
            part = pl.ds(j * length, length)
            flipped[i % 2, :, part] = rows[i // flips, part, at].T
        flip_copy(i).start()

    def found_copy(p, m):
        slot = p % 2
        return pltpu.make_async_copy(
            found.at[slot, m], results.at[m, :, columns(p, block)], found_sem.at[slot, m]
        )

    share = -(-capacity // parts)

    def heads(p, m):
        slot = p % 2

        @pl.when(jnp.logical_and(m == 0, p >= 2))
        def _():
            for i in range(parts):
                found_copy(p - 2, i).wait()

        def one(j):
            part = pl.ds(pl.multiple_of(j * length, length), length)
            alive = count > j
            for n in range(block // head_width):
                at = slice(n * head_width, (n + 1) * head_width)
                decay = mask[p * (block // head_width) + n]
                gain_row = gain[p, :, at]
                raw_query, raw_key = raw[slot, 0, part, at], raw[slot, 1, part, at]
                attended, kept = head_forward(
                    raw_query, raw_key, raw[slot, 2, part, at], decay, gain_row
                )
                grads = head_backward(
                    kept, raw_query, raw_key, raw[slot, 3, part, at], decay, gain_row
                )
                for i, result in enumerate((*grads, attended.astype(jnp.float32))):
                    found[slot, i, part, at] = jnp.where(alive, result, 0.0).astype(jnp.bfloat16)

        for i in range(share):
            j = m * share + i
            pl.when(j < capacity)(functools.partial(one, j))

        @pl.when(m == parts - 1)
        def _():
            for i in range(parts):
                found_copy(p, i).start()

    def product(s):
        m = s % parts
        p = s // parts
        source = jnp.where(m == parts - 1, 1, 0)

        def one(j):
            part = pl.ds(pl.multiple_of(j * length, length), length)
            weight = full[s].reshape(depth, block)
            raw[p % 2, m, part] = multiply(rows[source, part, :], weight, 1, 0)

        each(capacity, one)

    def step(t):
        pl.when(t > 0)(lambda: gather.tick(t))

        @pl.when(t < flip_ticks)
        def _():
            for i in range(flip_share):
                pl.when(t * flip_share + i < 2 * flips)(lambda i=i: flip(t * flip_share + i))

        s = t - gather.lag
        pl.when(s >= parts)(lambda: heads(s // parts - 1, s % parts))

        @pl.when(jnp.logical_and(s >= 0, s < steps))
        def _():
            gather.after_c(s)
            product(s)

    each(steps + parts + gather.lag, step)
    for i in range(2 * flips - 2, 2 * flips):
        flip_copy(i).wait()
    for p in range(max(pairs - 2, 0), pairs):
        for m in range(parts):
            found_copy(p, m).wait()
    gather.finish()


def replay(qkv_weight, out_weight, logged, cotangent, decay_logs, norm_gain, counts):
    helper_total = lax.axis_size("helper")
    parts, own, width = qkv_weight.shape[0] + 1, *out_weight.shape
    head_count, length = decay_logs.shape
    head_width = width // head_count
    block = head_width * (BLOCK_HEADS if head_count % BLOCK_HEADS == 0 else 1)
    steps = parts * (width // block)
    row_total, depth = logged.shape
    dma = pltpu.SemaphoreType.DMA
    whole = pl.BlockSpec(memory_space=pltpu.VMEM)
    away = pl.BlockSpec(memory_space=pl.ANY)
    return pl.pallas_call(
        functools.partial(replay_kernel, head_width),
        out_shape=[
            jax.ShapeDtypeStruct((parts, row_total, width), jnp.bfloat16),
            jax.ShapeDtypeStruct((2, depth, row_total), jnp.bfloat16),
        ],
        in_specs=[
            *[whole, whole, away, away, whole, whole],
            pl.BlockSpec(memory_space=pltpu.SMEM),
        ],
        out_specs=[away, away],
        scratch_shapes=[
            pltpu.VMEM((parts, own, width), jnp.bfloat16),
            pltpu.VMEM((head_count, length, length), jnp.float32),
            pltpu.VMEM((2, row_total, depth), jnp.bfloat16),
            pltpu.VMEM((steps, helper_total, own, block), jnp.bfloat16),
            pltpu.VMEM((2, parts, row_total, block), jnp.float32),
            pltpu.VMEM((2, parts, row_total, block), jnp.bfloat16),
            pltpu.VMEM((2, block, row_total), jnp.bfloat16),
            dma((2,)),
            dma((2, parts)),
            dma((2,)),
            *Gather.scratch(steps),
        ],
        compiler_params=pltpu.CompilerParams(
            collective_id=0, has_side_effects=True, vmem_limit_bytes=VMEM_LIMIT
        ),
    )(
        qkv_weight,
        out_weight,
        logged,
        cotangent,
        decay_logs,
        norm_gain.reshape(-1, 1, block),
        counts,
    )


def reduce_kernel(
    turned,
    results,
    qkv_weight_far,
    out_weight_far,
    qkv_first_far,
    out_first_far,
    qkv_second_far,
    out_second_far,
    pieces,
    qkv_moment,
    out_moment,
    left,
    right,
    own,
    core_out,
    core_in,
    own_x,
    x_out,
    x_in,
    own_z,
    z_out,
    z_in,
    left_sem,
    right_sem,
    c_send,
    c_recv,
    x_send,
    x_recv,
    z_send,
    z_recv,
    qkv_weight,
    out_weight,
    qkv_first,
    out_first,
    qkv_second,
    out_second,
    state_sem,
):
    states = [
        pltpu.make_async_copy(source, target, state_sem.at[i])
        for i, (source, target) in enumerate(
            (
                (qkv_weight_far, qkv_weight),
                (out_weight_far, out_weight),
                (qkv_first_far, qkv_first),
                (out_first_far, out_first),
                (qkv_second_far, qkv_second),
                (out_second_far, out_second),
            )
        )
    ]
    parts, _, width = results.shape
    block = right.shape[-1]
    pairs = width // block
    steps = parts * pairs
    size = out_weight.shape[0]
    _, (outer, inner, core), (z, x, c), _ = place()
    z_peer, x_peer, c_peer = helper_peers()

    def load_right(s):
        return pltpu.make_async_copy(
            results.at[s % parts, :, columns(s // parts, block)], right.at[s], right_sem.at[s]
        )

    def load_left(i):
        return pltpu.make_async_copy(turned.at[i], left.at[i], left_sem.at[i])

    load_left(0).start()
    load_right(0).start()
    for s in range(1, parts):
        load_right(s).start()
    load_left(1).start()
    for s in range(parts, steps):
        load_right(s).start()
    for state in states:
        state.start()
    greet(z_peer[1:] + x_peer[1:] + [c_peer])

    def c_copy(s):
        return remote(core_out.at[s % 2], core_in.at[s], c_send.at[s], c_recv.at[s], c_peer)

    def x_copy(s, j, r):
        mark = j * outer + r
        return remote(
            x_out.at[s % 2, j, r],
            x_in.at[s, j, r],
            x_send.at[s, mark],
            x_recv.at[s, mark],
            x_peer[j],
        )

    rounds = [*range(1, outer), 0]

    def z_copy(s, k):
        return remote(
            z_out.at[s % 2, k], z_in.at[s, k], z_send.at[s, k], z_recv.at[s, k], z_peer[k]
        )

    def begin(s):
        load_right(s).wait()
        pl.when(s == 0)(lambda: load_left(0).wait())
        pl.when(s == parts - 1)(lambda: load_left(1).wait())
        pl.when(s >= 2)(lambda: c_copy(s - 2).wait_send())
        source = jnp.where(s % parts == parts - 1, 1, 0)
        slot = s % 2

        def one(q):
            span = core * size
            part = pl.ds(pl.multiple_of(q * span, span), span)
            total = multiply(left[source, part, :], right[s], 1, 0)
            first, second = total[:size], total[size:]
            own[slot, q] = jnp.where(c == 0, first, second)
            core_out[slot, q] = jnp.where(c == 0, second, first).astype(jnp.bfloat16)

        each(outer * inner, one)
        c_copy(s).start()

    def after_c(s):
        c_copy(s).wait_recv()
        slot = s % 2

        @pl.when(s >= 2)
        def _():
            for j in range(1, inner):
                for r in rounds:
                    x_copy(s - 2, j, r).wait_send()

        for j in range(1, inner):
            for r in rounds:
                q = (z + r) % outer * inner + (x + j) % inner
                x_out[slot, j, r] = (own[slot, q] + core_in[s, q]).astype(jnp.bfloat16)
                x_copy(s, j, r).start()
        for r in rounds:
            q = (z + r) % outer * inner + x
            own_x[slot, r] = own[slot, q] + core_in[s, q]

    def after_x(s):
        slot = s % 2

        @pl.when(s >= 2)
        def _():
            for k in range(1, outer):
                z_copy(s - 2, k).wait_send()

        def total(r):
            value = own_x[slot, r]
            for j in range(1, inner):
                x_copy(s, j, r).wait_recv()
                value = value + x_in[s, j, r]
            return value

        for k in range(1, outer):
            z_out[slot, k] = total(k).astype(jnp.bfloat16)
            z_copy(s, k).start()
        own_z[slot] = total(0)

    def after_z(s):
        @pl.when(s == 0)
        def _():
            for state in states:
                state.wait()

        value = own_z[s % 2]
        for k in range(1, outer):
            z_copy(s, k).wait_recv()
            value = value + z_in[s, k]
        m = s % parts
        at = columns(s // parts, block)

        @pl.when(m < parts - 1)
        def _():
            piece, moment = adam_step(
                qkv_weight[m, :, at], qkv_first[m, :, at], qkv_second[m, :, at], value
            )
            pieces[m, :, at] = piece
            qkv_moment[m, :, at] = moment

        @pl.when(m == parts - 1)
        def _():
            piece, moment = adam_step(
                out_weight[:, at], out_first[:, at], out_second[:, at], value
            )
            pieces[m, :, at] = piece
            out_moment[:, at] = moment

    def step(t):
        for lag, body in enumerate((begin, after_c, after_x, after_z)):
            s = t - lag
            pl.when(jnp.logical_and(s >= 0, s < steps))(functools.partial(body, s))

    each(steps + 3, step)
    for s in range(max(steps - 2, 0), steps):
        c_copy(s).wait_send()
        for j in range(1, inner):
            for r in rounds:
                x_copy(s, j, r).wait_send()
        for k in range(1, outer):
            z_copy(s, k).wait_send()


def reduce_gradients(turned, results, states, head_count):
    helper_total = lax.axis_size("helper")
    outer, inner, core = grouping(helper_total)
    parts, row_total, width = results.shape
    depth = turned.shape[1]
    size = depth // helper_total
    block = width // head_count * (BLOCK_HEADS if head_count % BLOCK_HEADS == 0 else 1)
    steps = parts * (width // block)
    dma = pltpu.SemaphoreType.DMA
    half, full = jnp.bfloat16, jnp.float32
    tile = (size, block)
    whole = pl.BlockSpec(memory_space=pltpu.VMEM)
    away = pl.BlockSpec(memory_space=pl.ANY)
    return pl.pallas_call(
        reduce_kernel,
        out_shape=[
            jax.ShapeDtypeStruct((parts, size, width), half),
            jax.ShapeDtypeStruct((parts - 1, size, width), full),
            jax.ShapeDtypeStruct((size, width), full),
        ],
        in_specs=[away] * 8,
        out_specs=[whole] * 3,
        scratch_shapes=[
            pltpu.VMEM((2, depth, row_total), half),
            pltpu.VMEM((steps, row_total, block), half),
            pltpu.VMEM((2, outer * inner, *tile), full),
            pltpu.VMEM((2, outer * inner, *tile), half),
            pltpu.VMEM((steps, outer * inner, *tile), half),
            pltpu.VMEM((2, outer, *tile), full),
            pltpu.VMEM((2, inner, outer, *tile), half),
            pltpu.VMEM((steps, inner, outer, *tile), half),
            pltpu.VMEM((2, *tile), full),
            pltpu.VMEM((2, outer, *tile), half),
            pltpu.VMEM((steps, outer, *tile), half),
            dma((2,)),
            dma((steps,)),
            dma((steps,)),
            dma((steps,)),
            dma((steps, inner * outer)),
            dma((steps, inner * outer)),
            dma((steps, outer)),
            dma((steps, outer)),
            *[pltpu.VMEM(state.shape, state.dtype) for state in states],
            dma((len(states),)),
        ],
        compiler_params=pltpu.CompilerParams(
            collective_id=1, has_side_effects=True, vmem_limit_bytes=VMEM_LIMIT
        ),
    )(turned, results, *states)


def fresh_kernel(head_width, piece, fresh, decay_logs, gain, out, *scratch):
    exchange = out.dtype == fresh.dtype
    full, raw, mask, attended, total = scratch[:5]
    sems = scratch[5:]
    if exchange:
        other, other_attended, other_total, *marks = scratch[5:14]
        sems = scratch[14:]
    parts, _, width = piece.shape
    block = full.shape[-1]
    pairs = width // block
    steps = parts * pairs
    depth = fresh.shape[1]

    def piece_at(s):
        later = s - pairs
        m = jnp.where(later < 0, parts - 1, later % (parts - 1))
        p = jnp.where(later < 0, s, later // (parts - 1))
        return piece.at[m, :, columns(p, block)]

    gather = Gather(steps, piece_at, full, sems)
    greet(gather.peers(), exchange)
    gather.open()
    fill_mask(mask, decay_logs)
    total[...] = jnp.zeros_like(total)
    if exchange:
        other_total[...] = jnp.zeros_like(other_total)
        partner = 1 - lax.axis_index("tensor")
        y_send, y_recv, c_send, c_recv, a_send, a_recv = marks
        share = full.shape[1] // 2
        half = pl.ds(pl.multiple_of(gather.spot[2] * share, share), share)

        def y_copy(p):
            return remote(
                full.at[p, half], other.at[p, half], y_send.at[p], y_recv.at[p], partner, "tensor"
            )

        def c_copy(p):
            return remote(
                other.at[p, half], other.at[p, half], c_send.at[p], c_recv.at[p], gather.c_peer
            )

        def a_copy(p):
            return remote(
                attended.at[p], other_attended.at[p], a_send.at[p], a_recv.at[p], partner, "tensor"
            )

        def take_other(p):
            a_copy(p).wait_recv()
            c_copy(p).wait_recv()
            weight = other[p].reshape(depth, block)
            other_total[...] += multiply(other_attended[p], weight, 1, 1)

        def relay(i):
            y_copy(i).wait_recv()
            c_copy(i).start()

    def heads(p):
        for n in range(block // head_width):
            at = slice(n * head_width, (n + 1) * head_width)
            decay = mask[p * (block // head_width) + n]
            attended[p, :, at] = head_forward(
                raw[0, :, at], raw[1, :, at], raw[2, :, at], decay, gain[p, :, at]
            )[0]
        if exchange:
            a_copy(p).start()
        total[...] += multiply(attended[p], full[p].reshape(depth, block), 1, 1)
        if exchange:
            pl.when(p > 0)(lambda: take_other(p - 1))

    def compute(s):
        gather.after_c(s)
        if exchange:
            pl.when(s < pairs)(lambda: y_copy(s).start())
            since = s - 3
            turn = jnp.logical_and(since >= 0, since < 2 * pairs)
            pl.when(jnp.logical_and(turn, since % 2 == 0))(lambda: relay(since // 2))

        @pl.when(s >= pairs)
        def _():
            m = (s - pairs) % (parts - 1)
            raw[m] = multiply(fresh[...], full[s].reshape(depth, block), 1, 0)
            pl.when(m == parts - 2)(lambda: heads((s - pairs) // (parts - 1)))

    def step(t):
        pl.when(t > 0)(lambda: gather.tick(t))
        pl.when(t >= gather.lag)(lambda: compute(t - gather.lag))

    each(steps + gather.lag, step)
    if exchange:
        for p in range(pairs):
            if 3 + 2 * p >= steps:
                relay(p)
        take_other(pairs - 1)
        summed = total[...] + other_total[...]
        out[...] = (fresh[...].astype(jnp.float32) + summed).astype(out.dtype)
        for p in range(pairs):
            y_copy(p).wait_send()
            c_copy(p).wait_send()
            a_copy(p).wait_send()
    else:
        out[...] = total[...]
    gather.finish()


def fresh_forward(pieces, fresh, decay_logs, norm_gain):
    helper_total = lax.axis_size("helper")
    exchange = lax.axis_size("tensor") == 2
    parts, own, width = pieces.shape
    head_count, length = decay_logs.shape
    head_width = width // head_count
    block = head_width * (BLOCK_HEADS if head_count % BLOCK_HEADS == 0 else 1)
    pairs = width // block
    steps = parts * pairs
    row_total, depth = fresh.shape
    whole = pl.BlockSpec(memory_space=pltpu.VMEM)
    kind = fresh.dtype if exchange else jnp.float32
    total = pltpu.VMEM((row_total, own * helper_total), jnp.float32)
    attended = pltpu.VMEM((pairs, row_total, block), jnp.bfloat16)
    extra = [
        pltpu.VMEM((pairs, helper_total, own, block), jnp.bfloat16),
        attended,
        total,
        *[pltpu.SemaphoreType.DMA((pairs,))] * 6,
    ]
    return pl.pallas_call(
        functools.partial(fresh_kernel, head_width),
        out_shape=jax.ShapeDtypeStruct((row_total, own * helper_total), kind),
        in_specs=[whole] * 4,
        out_specs=whole,
        scratch_shapes=[
            pltpu.VMEM((steps, helper_total, own, block), jnp.bfloat16),
            pltpu.VMEM((parts - 1, row_total, block), jnp.float32),
            pltpu.VMEM((head_count, length, length), jnp.float32),
            attended,
            total,
            *(extra if exchange else []),
            *Gather.scratch(steps),
        ],
        compiler_params=pltpu.CompilerParams(
            collective_id=2, has_side_effects=True, vmem_limit_bytes=VMEM_LIMIT
        ),
    )(pieces, fresh, decay_logs, norm_gain.reshape(-1, 1, block))
def local(
    recorded_input_rows,
    out_cotangent,
    fresh_rows,
    seq_counts,
    decay_logs,
    norm_gain,
    qkv_weight,
    emitted_projection_matrix,
    qkv_first,
    qkv_second,
    out_first,
    out_second,
):
    head_count = decay_logs.shape[0]

    def parts_first(array):
        return jnp.transpose(array, (1, 0, 2))

    weight = parts_first(qkv_weight)

    results, turned = replay(
        weight,
        emitted_projection_matrix,
        recorded_input_rows,
        out_cotangent,
        decay_logs,
        norm_gain,
        seq_counts,
    )
    states = (
        weight,
        emitted_projection_matrix,
        parts_first(qkv_first),
        out_first,
        parts_first(qkv_second),
        out_second,
    )
    pieces, qkv_moment, out_moment = reduce_gradients(turned, results, states, head_count)
    fresh_out = fresh_forward(pieces, fresh_rows, decay_logs, norm_gain)
    if fresh_out.dtype != fresh_rows.dtype:
        fresh_out = finish(fresh_out, fresh_rows)
    return (fresh_out, parts_first(qkv_moment), out_moment)


def finish(partial_out, fresh):
    if lax.axis_size("tensor") == 2:
        width = partial_out.shape[1] // 2
        first = lax.axis_index("tensor") == 0
        left, right = partial_out[:, :width], partial_out[:, width:]
        came = swap(jnp.where(first, right, left).astype(jnp.bfloat16), "tensor", 1)
        residual = jnp.where(first, fresh[:, :width], fresh[:, width:])
        piece = residual.astype(jnp.float32) + (jnp.where(first, left, right) + came)
        piece = piece.astype(jnp.bfloat16)
        other = swap(piece, "tensor", 1)
        return jnp.concatenate(
            [jnp.where(first, piece, other), jnp.where(first, other, piece)], axis=1
        )
    share_sum = lax.psum_scatter(partial_out, "tensor", scatter_dimension=1, tiled=True)
    width = share_sum.shape[1]
    residual = lax.dynamic_slice_in_dim(fresh, lax.axis_index("tensor") * width, width, 1)
    piece = (residual.astype(jnp.float32) + share_sum).astype(jnp.bfloat16)
    return lax.all_gather(piece, "tensor", axis=1, tiled=True)


def solution(mesh):
    return jax.shard_map(
        local,
        mesh=mesh,
        in_specs=(
            P("helper", None),
            P("helper", None),
            P("helper", None),
            P(),
            P("tensor", None),
            P("tensor"),
            P("helper", None, "tensor"),
            P("helper", "tensor"),
            P("helper", None, "tensor"),
            P("helper", None, "tensor"),
            P("helper", "tensor"),
            P("helper", "tensor"),
        ),
        out_specs=(P("helper", None), P("helper", None, "tensor"), P("helper", "tensor")),
        check_vma=False,
    )
```

```python
import functools

import jax
import jax.numpy as jnp
from jax import lax
from jax.experimental import pallas as pl
from jax.experimental.pallas import tpu as pltpu
from jax.sharding import PartitionSpec as P


SEQ_LEN = 256


NORM_FLOOR = 1.0
BETA_ONE = 0.9
BETA_TWO = 0.95
ADAM_EPS = 1e-08
LEARN_RATE = 0.005
WEIGHT_DECAY = 0.1
BIAS_ONE = 0.9999734386011124
BIAS_TWO = 0.994079470779666


def multiply(left, right, left_dim, right_dim):
    return lax.dot_general(
        left, right, (((left_dim,), (right_dim,)), ((), ())), preferred_element_type=jnp.float32
    )


def head_forward(raw_query, raw_key, raw_value, mask, gain):
    sigma_query = jax.nn.sigmoid(raw_query)
    sigma_key = jax.nn.sigmoid(raw_key)
    queries = (raw_query * sigma_query).astype(jnp.bfloat16)
    key_rows = (raw_key * sigma_key).astype(jnp.bfloat16)
    values = raw_value.astype(jnp.bfloat16)
    weights = (multiply(queries, key_rows, 1, 1) * mask).astype(jnp.bfloat16)
    mixed = multiply(weights, values, 1, 0)
    mean_square = jnp.mean(mixed * mixed, axis=-1, keepdims=True)
    inverse = lax.rsqrt(jnp.maximum(mean_square, NORM_FLOOR))
    attended = (mixed * inverse * gain).astype(jnp.bfloat16)
    return (
        attended,
        (sigma_query, sigma_key, queries, key_rows, values, weights, mixed, mean_square, inverse),
    )


def adam_step(weight, first_moment, second_moment, gradient):
    first_new = BETA_ONE * first_moment + (1.0 - BETA_ONE) * gradient
    second_new = BETA_TWO * second_moment + (1.0 - BETA_TWO) * gradient * gradient
    update = first_new / BIAS_ONE / (jnp.sqrt(second_new / BIAS_TWO) + ADAM_EPS)
    weight_new = weight - LEARN_RATE * (update + WEIGHT_DECAY * weight)
    return (weight_new.astype(jnp.bfloat16), first_new)


def swap(value, axis, distance):
    count = lax.axis_size(axis)
    return lax.ppermute(value, axis, [(i, i ^ distance) for i in range(count)])


def grouping(count):
    core = 2
    inner = 2
    return count // (core * inner), inner, core


VMEM_LIMIT = 66_000_000
BLOCK_HEADS = 2


def place():
    helper_total = lax.axis_size("helper")
    outer, inner, core = grouping(helper_total)
    helper = lax.axis_index("helper")
    z = helper // (inner * core)
    x = (helper // core) % inner
    c = helper % core

    def at(zz, xx, cc):
        return (zz * inner + xx) * core + cc

    return helper, (outer, inner, core), (z, x, c), at


def remote(source, target, send, recv, peer, axis="helper"):
    return pltpu.make_async_remote_copy(
        src_ref=source,
        dst_ref=target,
        send_sem=send,
        recv_sem=recv,
        device_id={axis: peer},
        device_id_type=pl.DeviceIdType.MESH,
    )


def greet(peers, across=False):
    barrier = pltpu.get_barrier_semaphore()
    targets = [{"helper": peer} for peer in peers]
    if across:
        targets.append({"tensor": 1 - lax.axis_index("tensor")})
    for target in targets:
        pl.semaphore_signal(
            barrier, inc=1, device_id=target, device_id_type=pl.DeviceIdType.MESH
        )
    pl.semaphore_wait(barrier, len(targets))


def line_orders():
    _, (outer, _, _), (z, _, _), _ = place()
    if outer != 4:
        return [list(range(1, outer))] * 2
    low, high = z == 0, z == outer - 1
    end = jnp.logical_or(low, high)
    first = jnp.where(low, 3, 1)
    last = jnp.where(low, 1, 3)
    far = [jnp.where(end, first, 2), jnp.where(end, 2, 1), jnp.where(end, last, 3)]
    near = [jnp.where(low, 3, 1), jnp.where(end, 2, 3), jnp.where(low, 1, jnp.where(high, 3, 2))]
    return far, near


def helper_peers():
    _, (outer, inner, _), (z, x, c), at = place()

    def z_peer(k):
        return at((z + k) % outer, x, c)

    x_peer = [None] + [at(z, (x + j) % inner, c) for j in range(1, inner)]
    return z_peer, x_peer, at(z, x, 1 - c)


def each(count, body):
    lax.fori_loop(0, count, lambda i, carry: (body(i), carry)[1], 0)


class Gather:
    def __init__(self, steps, piece_at, full, sems):
        self.steps, self.piece_at, self.full = steps, piece_at, full
        self.z_send, self.z_recv, self.x_send, self.x_recv, self.c_send, self.c_recv = sems
        self.helper, (self.outer, self.inner, _), self.spot, self.at = place()
        self.z_peer, self.x_peer, self.c_peer = helper_peers()
        self.far, self.near = line_orders()

    @staticmethod
    def scratch(steps):
        outer, inner, _ = grouping(lax.axis_size("helper"))
        sizes = [outer, outer, inner * outer, inner * outer, inner * outer, inner * outer]
        return [pltpu.SemaphoreType.DMA((steps, size)) for size in sizes]

    def peers(self):
        z_peers = [self.z_peer(k) for k in range(1, self.outer)]
        return z_peers + self.x_peer[1:] + [self.c_peer]

    def owner(self, j, k):
        z, x, c = self.spot
        return self.at((z + self.outer - k) % self.outer, (x + self.inner - j) % self.inner, c)

    def source(self, s, j, k):
        own = isinstance(k, int) and k == 0 and j == 0
        return self.piece_at(s) if own else self.full.at[s, self.owner(j, k)]

    def z_copy(self, s, k):
        return remote(
            self.piece_at(s),
            self.full.at[s, self.helper],
            self.z_send.at[s, k],
            self.z_recv.at[s, k],
            self.z_peer(k),
        )

    def x_copy(self, s, j, k):
        slot = j * self.outer + k
        return remote(
            self.source(s, 0, k),
            self.full.at[s, self.owner(0, k)],
            self.x_send.at[s, slot],
            self.x_recv.at[s, slot],
            self.x_peer[j],
        )

    def c_copy(self, s, j, k):
        slot = j * self.outer + k
        return remote(
            self.source(s, j, k),
            self.full.at[s, self.owner(j, k)],
            self.c_send.at[s, slot],
            self.c_recv.at[s, slot],
            self.c_peer,
        )

    lag = 2
    ahead = 3

    def stage(self, s, body):
        pl.when(jnp.logical_and(s >= 0, s < self.steps))(lambda: body(s))

    def begin(self, s):
        for k in self.far:
            self.z_copy(s, k).start()
        self.c_copy(s, 0, 0).start()
        self.full[s, self.helper] = self.piece_at(s)[...]

    def begin_x(self, s):
        for j in range(1, self.inner):
            self.x_copy(s, j, 0).start()

    def open(self):
        self.stage(0, self.begin)
        for s in range(self.ahead + 1):
            self.stage(s, self.begin_x)
        self.stage(1, self.begin)

    def after_z(self, s):
        for k in self.near:
            self.z_copy(s, k).wait_recv()
            for j in range(1, self.inner):
                self.x_copy(s, j, k).start()
            self.c_copy(s, 0, k).start()

    def after_x(self, s):
        for k in [0, *self.near]:
            for j in range(1, self.inner):
                self.x_copy(s, j, k).wait_recv()
                self.c_copy(s, j, k).start()

    def after_c(self, s):
        for k in range(self.outer):
            for j in range(self.inner):
                self.c_copy(s, j, k).wait_recv()

    def tick(self, t):
        self.stage(t + 1, self.begin)
        self.stage(t + self.ahead, self.begin_x)
        self.stage(t - 1, self.after_z)
        self.stage(t - 2, self.after_x)

    def finish(self):
        def drain(s):
            for k in range(self.outer):
                if k:
                    self.z_copy(s, k).wait_send()
                for j in range(self.inner):
                    if j:
                        self.x_copy(s, j, k).wait_send()
                    self.c_copy(s, j, k).wait_send()

        each(self.steps, drain)


def columns(p, width):
    return pl.ds(pl.multiple_of(p * width, width), width)


def fill_mask(mask, decay_logs):
    length = mask.shape[1]
    down = lax.broadcasted_iota(jnp.int32, (length, length), 0)
    across = lax.broadcasted_iota(jnp.int32, (length, length), 1)
    later = down >= across
    for n in range(mask.shape[0]):
        logs = jnp.broadcast_to(decay_logs[n : n + 1, :], (length, length))
        running = jnp.sum(jnp.where(later, logs, 0.0), axis=1, keepdims=True)
        running = jnp.broadcast_to(running, (length, length))
        turned = jnp.sum(jnp.where(down == across, running, 0.0), axis=0, keepdims=True)
        spread_factor = running - turned
        mask[n] = jnp.where(later, jnp.exp(jnp.where(later, spread_factor, 0.0)), 0.0)


def head_backward(kept, raw_query, raw_key, cotangent, decay, gain_row):
    sigma_query, sigma_key, queries, key_rows, values, weights, mixed, square, inverse = kept
    active = jnp.where(square > NORM_FLOOR, 1.0, 0.0)
    scaled = cotangent * gain_row
    grad_mixed = inverse * scaled - active * mixed * (inverse * inverse * inverse) * jnp.mean(
        scaled * mixed, axis=-1, keepdims=True
    )
    grad_mixed = grad_mixed.astype(jnp.bfloat16)
    grad_scores = (multiply(grad_mixed, values, 1, 1) * decay).astype(jnp.bfloat16)
    grad_value = multiply(weights, grad_mixed, 0, 0)
    grad_query = multiply(grad_scores, key_rows, 1, 0)
    grad_key = multiply(grad_scores, queries, 0, 0)
    grad_query = grad_query * sigma_query * (1.0 + raw_query * (1.0 - sigma_query))
    grad_key = grad_key * sigma_key * (1.0 + raw_key * (1.0 - sigma_key))
    return grad_query, grad_key, grad_value


def replay_kernel(
    head_width,
    qkv_weight,
    out_weight,
    logged,
    cotangent,
    decay_logs,
    gain,
    counts,
    results,
    turned,
    piece,
    mask,
    rows,
    full,
    raw,
    found,
    flipped,
    row_sem,
    found_sem,
    flip_sem,
    *sems,
):
    parts, _, width = piece.shape
    block = full.shape[-1]
    pairs = width // block
    steps = parts * pairs
    length = mask.shape[1]
    depth = rows.shape[2]
    capacity = rows.shape[1] // length
    count = jnp.full((1, head_width), counts[lax.axis_index("helper")], jnp.int32)
    gather = Gather(steps, lambda s: piece.at[s % parts, :, columns(s // parts, block)], full, sems)
    loads = [
        pltpu.make_async_copy(source, rows.at[i], row_sem.at[i])
        for i, source in enumerate((logged, cotangent))
    ]
    for load in loads:
        load.start()
    for m in range(parts - 1):
        piece[m] = qkv_weight[m].astype(jnp.bfloat16)
    piece[parts - 1] = out_weight[...].astype(jnp.bfloat16)
    greet(gather.peers())
    gather.open()
    fill_mask(mask, decay_logs)
    for load in loads:
        load.wait()

    flips = depth // block
    flip_ticks = 4
    flip_share = -(-2 * flips // flip_ticks)

    def flip_copy(i):
        slot = i % 2
        return pltpu.make_async_copy(
            flipped.at[slot],
            turned.at[i // flips, columns(i % flips, block)],
            flip_sem.at[slot],
        )

    def flip(i):
        pl.when(i >= 2)(lambda: flip_copy(i - 2).wait())
        at = columns(i % flips, block)
        for j in range(capacity):
            part = pl.ds(j * length, length)
            flipped[i % 2, :, part] = rows[i // flips, part, at].T
        flip_copy(i).start()

    def found_copy(p, m):
        slot = p % 2
        return pltpu.make_async_copy(
            found.at[slot, m], results.at[m, :, columns(p, block)], found_sem.at[slot, m]
        )

    share = -(-capacity // parts)

    def heads(p, m):
        slot = p % 2

        @pl.when(jnp.logical_and(m == 0, p >= 2))
        def _():
            for i in range(parts):
                found_copy(p - 2, i).wait()

        def one(j):
            part = pl.ds(pl.multiple_of(j * length, length), length)
            alive = count > j
            for n in range(block // head_width):
                at = slice(n * head_width, (n + 1) * head_width)
                decay = mask[p * (block // head_width) + n]
                gain_row = gain[p, :, at]
                raw_query, raw_key = raw[slot, 0, part, at], raw[slot, 1, part, at]
                attended, kept = head_forward(
                    raw_query, raw_key, raw[slot, 2, part, at], decay, gain_row
                )
                grads = head_backward(
                    kept, raw_query, raw_key, raw[slot, 3, part, at], decay, gain_row
                )
                for i, result in enumerate((*grads, attended.astype(jnp.float32))):
                    found[slot, i, part, at] = jnp.where(alive, result, 0.0).astype(jnp.bfloat16)

        for i in range(share):
            j = m * share + i
            pl.when(j < capacity)(functools.partial(one, j))

        @pl.when(m == parts - 1)
        def _():
            for i in range(parts):
                found_copy(p, i).start()

    def product(s):
        m = s % parts
        p = s // parts
        source = jnp.where(m == parts - 1, 1, 0)

        def one(j):
            part = pl.ds(pl.multiple_of(j * length, length), length)
            weight = full[s].reshape(depth, block)
            raw[p % 2, m, part] = multiply(rows[source, part, :], weight, 1, 0)

        each(capacity, one)

    def step(t):
        pl.when(t > 0)(lambda: gather.tick(t))

        @pl.when(t < flip_ticks)
        def _():
            for i in range(flip_share):
                pl.when(t * flip_share + i < 2 * flips)(lambda i=i: flip(t * flip_share + i))

        s = t - gather.lag
        pl.when(s >= parts)(lambda: heads(s // parts - 1, s % parts))

        @pl.when(jnp.logical_and(s >= 0, s < steps))
        def _():
            gather.after_c(s)
            product(s)

    each(steps + parts + gather.lag, step)
    for i in range(2 * flips - 2, 2 * flips):
        flip_copy(i).wait()
    for p in range(max(pairs - 2, 0), pairs):
        for m in range(parts):
            found_copy(p, m).wait()
    gather.finish()


def replay(qkv_weight, out_weight, logged, cotangent, decay_logs, norm_gain, counts):
    helper_total = lax.axis_size("helper")
    parts, own, width = qkv_weight.shape[0] + 1, *out_weight.shape
    head_count, length = decay_logs.shape
    head_width = width // head_count
    block = head_width * (BLOCK_HEADS if head_count % BLOCK_HEADS == 0 else 1)
    steps = parts * (width // block)
    row_total, depth = logged.shape
    dma = pltpu.SemaphoreType.DMA
    whole = pl.BlockSpec(memory_space=pltpu.VMEM)
    away = pl.BlockSpec(memory_space=pl.ANY)
    return pl.pallas_call(
        functools.partial(replay_kernel, head_width),
        out_shape=[
            jax.ShapeDtypeStruct((parts, row_total, width), jnp.bfloat16),
            jax.ShapeDtypeStruct((2, depth, row_total), jnp.bfloat16),
        ],
        in_specs=[
            *[whole, whole, away, away, whole, whole],
            pl.BlockSpec(memory_space=pltpu.SMEM),
        ],
        out_specs=[away, away],
        scratch_shapes=[
            pltpu.VMEM((parts, own, width), jnp.bfloat16),
            pltpu.VMEM((head_count, length, length), jnp.float32),
            pltpu.VMEM((2, row_total, depth), jnp.bfloat16),
            pltpu.VMEM((steps, helper_total, own, block), jnp.bfloat16),
            pltpu.VMEM((2, parts, row_total, block), jnp.float32),
            pltpu.VMEM((2, parts, row_total, block), jnp.bfloat16),
            pltpu.VMEM((2, block, row_total), jnp.bfloat16),
            dma((2,)),
            dma((2, parts)),
            dma((2,)),
            *Gather.scratch(steps),
        ],
        compiler_params=pltpu.CompilerParams(
            collective_id=0, has_side_effects=True, vmem_limit_bytes=VMEM_LIMIT
        ),
    )(
        qkv_weight,
        out_weight,
        logged,
        cotangent,
        decay_logs,
        norm_gain.reshape(-1, 1, block),
        counts,
    )


def reduce_kernel(
    turned,
    results,
    qkv_weight_far,
    out_weight_far,
    qkv_first_far,
    out_first_far,
    qkv_second_far,
    out_second_far,
    pieces,
    qkv_moment,
    out_moment,
    left,
    right,
    own,
    core_out,
    core_in,
    own_x,
    x_out,
    x_in,
    own_z,
    z_out,
    z_in,
    left_sem,
    right_sem,
    c_send,
    c_recv,
    x_send,
    x_recv,
    z_send,
    z_recv,
    qkv_weight,
    out_weight,
    qkv_first,
    out_first,
    qkv_second,
    out_second,
    state_sem,
):
    states = [
        pltpu.make_async_copy(source, target, state_sem.at[i])
        for i, (source, target) in enumerate(
            (
                (qkv_weight_far, qkv_weight),
                (out_weight_far, out_weight),
                (qkv_first_far, qkv_first),
                (out_first_far, out_first),
                (qkv_second_far, qkv_second),
                (out_second_far, out_second),
            )
        )
    ]
    parts, _, width = results.shape
    block = right.shape[-1]
    pairs = width // block
    steps = parts * pairs
    size = out_weight.shape[0]
    _, (outer, inner, core), (z, x, c), _ = place()
    z_peer, x_peer, c_peer = helper_peers()

    def load_right(s):
        return pltpu.make_async_copy(
            results.at[s % parts, :, columns(s // parts, block)], right.at[s], right_sem.at[s]
        )

    def load_left(i):
        return pltpu.make_async_copy(turned.at[i], left.at[i], left_sem.at[i])

    load_left(0).start()
    load_right(0).start()
    for s in range(1, parts):
        load_right(s).start()
    load_left(1).start()
    for s in range(parts, steps):
        load_right(s).start()
    for state in states:
        state.start()
    greet([z_peer(k) for k in range(1, outer)] + x_peer[1:] + [c_peer])
    far, _ = line_orders()

    def c_copy(s):
        return remote(core_out.at[s % 2], core_in.at[s], c_send.at[s], c_recv.at[s], c_peer)

    def x_copy(s, j, r):
        mark = j * outer + r
        return remote(
            x_out.at[s % 2, j, r],
            x_in.at[s, j, r],
            x_send.at[s, mark],
            x_recv.at[s, mark],
            x_peer[j],
        )

    rounds = [*far, 0]

    def z_copy(s, k):
        return remote(
            z_out.at[s % 2, k], z_in.at[s, k], z_send.at[s, k], z_recv.at[s, k], z_peer(k)
        )

    def begin(s):
        load_right(s).wait()
        pl.when(s == 0)(lambda: load_left(0).wait())
        pl.when(s == parts - 1)(lambda: load_left(1).wait())
        pl.when(s >= 2)(lambda: c_copy(s - 2).wait_send())
        source = jnp.where(s % parts == parts - 1, 1, 0)
        slot = s % 2

        def one(q):
            span = core * size
            part = pl.ds(pl.multiple_of(q * span, span), span)
            total = multiply(left[source, part, :], right[s], 1, 0)
            first, second = total[:size], total[size:]
            own[slot, q] = jnp.where(c == 0, first, second)
            core_out[slot, q] = jnp.where(c == 0, second, first).astype(jnp.bfloat16)

        each(outer * inner, one)
        c_copy(s).start()

    def after_c(s):
        c_copy(s).wait_recv()
        slot = s % 2

        @pl.when(s >= 2)
        def _():
            for j in range(1, inner):
                for r in rounds:
                    x_copy(s - 2, j, r).wait_send()

        for j in range(1, inner):
            for r in rounds:
                q = (z + r) % outer * inner + (x + j) % inner
                x_out[slot, j, r] = (own[slot, q] + core_in[s, q]).astype(jnp.bfloat16)
                x_copy(s, j, r).start()
        for r in rounds:
            q = (z + r) % outer * inner + x
            own_x[slot, r] = own[slot, q] + core_in[s, q]

    def after_x(s):
        slot = s % 2

        @pl.when(s >= 2)
        def _():
            for k in range(1, outer):
                z_copy(s - 2, k).wait_send()

        def total(r):
            value = own_x[slot, r]
            for j in range(1, inner):
                x_copy(s, j, r).wait_recv()
                value = value + x_in[s, j, r]
            return value

        for k in far:
            z_out[slot, k] = total(k).astype(jnp.bfloat16)
            z_copy(s, k).start()
        own_z[slot] = total(0)

    def after_z(s):
        @pl.when(s == 0)
        def _():
            for state in states:
                state.wait()

        value = own_z[s % 2]
        for k in range(1, outer):
            z_copy(s, k).wait_recv()
            value = value + z_in[s, k]
        m = s % parts
        at = columns(s // parts, block)

        @pl.when(m < parts - 1)
        def _():
            piece, moment = adam_step(
                qkv_weight[m, :, at], qkv_first[m, :, at], qkv_second[m, :, at], value
            )
            pieces[m, :, at] = piece
            qkv_moment[m, :, at] = moment

        @pl.when(m == parts - 1)
        def _():
            piece, moment = adam_step(
                out_weight[:, at], out_first[:, at], out_second[:, at], value
            )
            pieces[m, :, at] = piece
            out_moment[:, at] = moment

    def step(t):
        for lag, body in enumerate((begin, after_c, after_x, after_z)):
            s = t - lag
            pl.when(jnp.logical_and(s >= 0, s < steps))(functools.partial(body, s))

    each(steps + 3, step)
    for s in range(max(steps - 2, 0), steps):
        c_copy(s).wait_send()
        for j in range(1, inner):
            for r in rounds:
                x_copy(s, j, r).wait_send()
        for k in range(1, outer):
            z_copy(s, k).wait_send()


def reduce_gradients(turned, results, states, head_count):
    helper_total = lax.axis_size("helper")
    outer, inner, core = grouping(helper_total)
    parts, row_total, width = results.shape
    depth = turned.shape[1]
    size = depth // helper_total
    block = width // head_count * (BLOCK_HEADS if head_count % BLOCK_HEADS == 0 else 1)
    steps = parts * (width // block)
    dma = pltpu.SemaphoreType.DMA
    half, full = jnp.bfloat16, jnp.float32
    tile = (size, block)
    whole = pl.BlockSpec(memory_space=pltpu.VMEM)
    away = pl.BlockSpec(memory_space=pl.ANY)
    return pl.pallas_call(
        reduce_kernel,
        out_shape=[
            jax.ShapeDtypeStruct((parts, size, width), half),
            jax.ShapeDtypeStruct((parts - 1, size, width), full),
            jax.ShapeDtypeStruct((size, width), full),
        ],
        in_specs=[away] * 8,
        out_specs=[whole] * 3,
        scratch_shapes=[
            pltpu.VMEM((2, depth, row_total), half),
            pltpu.VMEM((steps, row_total, block), half),
            pltpu.VMEM((2, outer * inner, *tile), full),
            pltpu.VMEM((2, outer * inner, *tile), half),
            pltpu.VMEM((steps, outer * inner, *tile), half),
            pltpu.VMEM((2, outer, *tile), full),
            pltpu.VMEM((2, inner, outer, *tile), half),
            pltpu.VMEM((steps, inner, outer, *tile), half),
            pltpu.VMEM((2, *tile), full),
            pltpu.VMEM((2, outer, *tile), half),
            pltpu.VMEM((steps, outer, *tile), half),
            dma((2,)),
            dma((steps,)),
            dma((steps,)),
            dma((steps,)),
            dma((steps, inner * outer)),
            dma((steps, inner * outer)),
            dma((steps, outer)),
            dma((steps, outer)),
            *[pltpu.VMEM(state.shape, state.dtype) for state in states],
            dma((len(states),)),
        ],
        compiler_params=pltpu.CompilerParams(
            collective_id=1, has_side_effects=True, vmem_limit_bytes=VMEM_LIMIT
        ),
    )(turned, results, *states)


def fresh_kernel(head_width, piece, fresh, decay_logs, gain, out, *scratch):
    exchange = out.dtype == fresh.dtype
    full, raw, mask, attended, total = scratch[:5]
    sems = scratch[5:]
    if exchange:
        other, other_attended, other_total, *marks = scratch[5:14]
        sems = scratch[14:]
    parts, _, width = piece.shape
    block = full.shape[-1]
    pairs = width // block
    steps = parts * pairs
    depth = fresh.shape[1]

    def piece_at(s):
        later = s - pairs
        m = jnp.where(later < 0, parts - 1, later % (parts - 1))
        p = jnp.where(later < 0, s, later // (parts - 1))
        return piece.at[m, :, columns(p, block)]

    gather = Gather(steps, piece_at, full, sems)
    greet(gather.peers(), exchange)
    gather.open()
    fill_mask(mask, decay_logs)
    total[...] = jnp.zeros_like(total)
    if exchange:
        other_total[...] = jnp.zeros_like(other_total)
        partner = 1 - lax.axis_index("tensor")
        y_send, y_recv, c_send, c_recv, a_send, a_recv = marks
        share = full.shape[1] // 2
        half = pl.ds(pl.multiple_of(gather.spot[2] * share, share), share)

        def y_copy(p):
            return remote(
                full.at[p, half], other.at[p, half], y_send.at[p], y_recv.at[p], partner, "tensor"
            )

        def c_copy(p):
            return remote(
                other.at[p, half], other.at[p, half], c_send.at[p], c_recv.at[p], gather.c_peer
            )

        def a_copy(p):
            return remote(
                attended.at[p], other_attended.at[p], a_send.at[p], a_recv.at[p], partner, "tensor"
            )

        def take_other(p):
            a_copy(p).wait_recv()
            c_copy(p).wait_recv()
            weight = other[p].reshape(depth, block)
            other_total[...] += multiply(other_attended[p], weight, 1, 1)

        def relay(i):
            y_copy(i).wait_recv()
            c_copy(i).start()

    def heads(p):
        for n in range(block // head_width):
            at = slice(n * head_width, (n + 1) * head_width)
            decay = mask[p * (block // head_width) + n]
            attended[p, :, at] = head_forward(
                raw[0, :, at], raw[1, :, at], raw[2, :, at], decay, gain[p, :, at]
            )[0]
        if exchange:
            a_copy(p).start()
        total[...] += multiply(attended[p], full[p].reshape(depth, block), 1, 1)
        if exchange:
            pl.when(p > 0)(lambda: take_other(p - 1))

    def compute(s):
        gather.after_c(s)
        if exchange:
            pl.when(s < pairs)(lambda: y_copy(s).start())
            since = s - 3
            turn = jnp.logical_and(since >= 0, since < 2 * pairs)
            pl.when(jnp.logical_and(turn, since % 2 == 0))(lambda: relay(since // 2))

        @pl.when(s >= pairs)
        def _():
            m = (s - pairs) % (parts - 1)
            raw[m] = multiply(fresh[...], full[s].reshape(depth, block), 1, 0)
            pl.when(m == parts - 2)(lambda: heads((s - pairs) // (parts - 1)))

    def step(t):
        pl.when(t > 0)(lambda: gather.tick(t))
        pl.when(t >= gather.lag)(lambda: compute(t - gather.lag))

    each(steps + gather.lag, step)
    if exchange:
        for p in range(pairs):
            if 3 + 2 * p >= steps:
                relay(p)
        take_other(pairs - 1)
        summed = total[...] + other_total[...]
        out[...] = (fresh[...].astype(jnp.float32) + summed).astype(out.dtype)
        for p in range(pairs):
            y_copy(p).wait_send()
            c_copy(p).wait_send()
            a_copy(p).wait_send()
    else:
        out[...] = total[...]
    gather.finish()


def fresh_forward(pieces, fresh, decay_logs, norm_gain):
    helper_total = lax.axis_size("helper")
    exchange = lax.axis_size("tensor") == 2
    parts, own, width = pieces.shape
    head_count, length = decay_logs.shape
    head_width = width // head_count
    block = head_width * (BLOCK_HEADS if head_count % BLOCK_HEADS == 0 else 1)
    pairs = width // block
    steps = parts * pairs
    row_total, depth = fresh.shape
    whole = pl.BlockSpec(memory_space=pltpu.VMEM)
    kind = fresh.dtype if exchange else jnp.float32
    total = pltpu.VMEM((row_total, own * helper_total), jnp.float32)
    attended = pltpu.VMEM((pairs, row_total, block), jnp.bfloat16)
    extra = [
        pltpu.VMEM((pairs, helper_total, own, block), jnp.bfloat16),
        attended,
        total,
        *[pltpu.SemaphoreType.DMA((pairs,))] * 6,
    ]
    return pl.pallas_call(
        functools.partial(fresh_kernel, head_width),
        out_shape=jax.ShapeDtypeStruct((row_total, own * helper_total), kind),
        in_specs=[whole] * 4,
        out_specs=whole,
        scratch_shapes=[
            pltpu.VMEM((steps, helper_total, own, block), jnp.bfloat16),
            pltpu.VMEM((parts - 1, row_total, block), jnp.float32),
            pltpu.VMEM((head_count, length, length), jnp.float32),
            attended,
            total,
            *(extra if exchange else []),
            *Gather.scratch(steps),
        ],
        compiler_params=pltpu.CompilerParams(
            collective_id=2, has_side_effects=True, vmem_limit_bytes=VMEM_LIMIT
        ),
    )(pieces, fresh, decay_logs, norm_gain.reshape(-1, 1, block))
def local(
    recorded_input_rows,
    out_cotangent,
    fresh_rows,
    seq_counts,
    decay_logs,
    norm_gain,
    qkv_weight,
    emitted_projection_matrix,
    qkv_first,
    qkv_second,
    out_first,
    out_second,
):
    head_count = decay_logs.shape[0]

    def parts_first(array):
        return jnp.transpose(array, (1, 0, 2))

    weight = parts_first(qkv_weight)

    results, turned = replay(
        weight,
        emitted_projection_matrix,
        recorded_input_rows,
        out_cotangent,
        decay_logs,
        norm_gain,
        seq_counts,
    )
    states = (
        weight,
        emitted_projection_matrix,
        parts_first(qkv_first),
        out_first,
        parts_first(qkv_second),
        out_second,
    )
    pieces, qkv_moment, out_moment = reduce_gradients(turned, results, states, head_count)
    fresh_out = fresh_forward(pieces, fresh_rows, decay_logs, norm_gain)
    if fresh_out.dtype != fresh_rows.dtype:
        fresh_out = finish(fresh_out, fresh_rows)
    return (fresh_out, parts_first(qkv_moment), out_moment)


def finish(partial_out, fresh):
    if lax.axis_size("tensor") == 2:
        width = partial_out.shape[1] // 2
        first = lax.axis_index("tensor") == 0
        left, right = partial_out[:, :width], partial_out[:, width:]
        came = swap(jnp.where(first, right, left).astype(jnp.bfloat16), "tensor", 1)
        residual = jnp.where(first, fresh[:, :width], fresh[:, width:])
        piece = residual.astype(jnp.float32) + (jnp.where(first, left, right) + came)
        piece = piece.astype(jnp.bfloat16)
        other = swap(piece, "tensor", 1)
        return jnp.concatenate(
            [jnp.where(first, piece, other), jnp.where(first, other, piece)], axis=1
        )
    share_sum = lax.psum_scatter(partial_out, "tensor", scatter_dimension=1, tiled=True)
    width = share_sum.shape[1]
    residual = lax.dynamic_slice_in_dim(fresh, lax.axis_index("tensor") * width, width, 1)
    piece = (residual.astype(jnp.float32) + share_sum).astype(jnp.bfloat16)
    return lax.all_gather(piece, "tensor", axis=1, tiled=True)


def solution(mesh):
    return jax.shard_map(
        local,
        mesh=mesh,
        in_specs=(
            P("helper", None),
            P("helper", None),
            P("helper", None),
            P(),
            P("tensor", None),
            P("tensor"),
            P("helper", None, "tensor"),
            P("helper", "tensor"),
            P("helper", None, "tensor"),
            P("helper", None, "tensor"),
            P("helper", "tensor"),
            P("helper", "tensor"),
        ),
        out_specs=(P("helper", None), P("helper", None, "tensor"), P("helper", "tensor")),
        check_vma=False,
    )
```
